32 devices in a mesh: groups: 2 (over y), blk: 8 (over z, x), rep: 2 (over core).
Axes of the slice: x: 2, y: 2, z: 4, core: 2. Of those that a mesh axis runs over, the one named last changes fastest.
Arguments:
- tokens: bfloat16 [16384, 1024], P(('groups', 'blk', 'rep')), parts along dimension 0, may hold values from -6 to 6
- hidden_grad: bfloat16 [16384, 4096], P(('groups', 'blk', 'rep')), parts along dimension 0, may hold values from -6 to 6
- weights: bfloat16 [2, 4096, 1024], P(None, 'blk', 'rep'), may hold values from -0.1875 to 0.1875
- first_moment: float32 [2, 8192, 1024], P(None, ('groups', 'blk'), 'rep'), parts along dimension 1, may hold values from -0.0014648438 to 0.0014648438
- second_moment: float32 [2, 8192, 1024], P(None, ('groups', 'blk'), 'rep'), parts along dimension 1, may hold values from 1e-09 to 1e-07
Outputs:
- hidden: bfloat16 [16384, 4096], P(('groups', 'blk', 'rep')), parts along dimension 0
- adam_step: float32 [2, 8192, 1024], P(None, ('groups', 'blk')), parts along dimension 1
The draws below stay inside these ranges and needn't reach their ends.
There are 2 independent parts, one for each index of `groups`. The reference program is written for one: setup_inputs(seed, part) draws one part's arguments, and reference() takes and returns one part's arrays. A program takes and returns all parts, laid end to end along the dimension named above; an argument that names none is the same for every part. Nothing has to cross between parts.
All inputs are finite; a program needn't handle non-finite values.
Results may differ from the reference program's by a relative error of at most 0.0034.
Values may be sent and summed in bfloat16 or wider, within the bound.
A program may use at most 128 MiB of HBM per device.

```python
import math
import jax
import jax.numpy as jnp
from jax import lax

D = 1024
FW = 4096
TOK_DEV = 512
PANEL = 512
WINDOW = 8
TOKENS = 8192
N_BLK = 8
N_REP = 2


def levels(stream_key, shape, shards, least, top_value):
    loudness, own = 1.0, jax.random.fold_in(stream_key, 6)
    for position, parts in shards:
        steps = jnp.exp(jax.random.uniform(jax.random.fold_in(own, position), (parts,), jnp.float32, least / len(shards), top_value / len(shards)))
        loudness = loudness * jnp.repeat(steps, shape[position] // parts).reshape([-1 if axis == position else 1 for axis in range(len(shape))])
    return loudness


def gaussian(rng, shape, scale, bound, cuts=(), held_as=jnp.bfloat16):
    loudness = levels(rng, shape, cuts, -0.22, 0.18) if cuts else 1.0
    result = jax.random.normal(rng, shape, jnp.float32) * scale * loudness
    return jnp.minimum(jnp.maximum(result, -bound), bound).astype(held_as)


def setup_inputs(seed: int = 0, part: int = 0) -> dict:
    keys = jax.random.split(jax.random.key(seed), 6)
    part_splits = jax.random.split(jax.random.fold_in(keys[5], part), 6)
    tokens = gaussian(part_splits[0], (TOKENS, D), 1.0, 6.0, ((0, 16),))
    hidden_grad = gaussian(part_splits[1], (TOKENS, WINDOW * PANEL), 1.0, 6.0, ((0, 16),))
    weights = gaussian(keys[2], (2, FW, D), D ** -0.5, 0.1875, ((1, 8), (2, 2)))
    first_moment = gaussian(part_splits[3], (2, FW, D), 0.0001, 0.0014648438, ((1, 8), (2, 2)), jnp.float32)
    second_moment = jnp.clip(jnp.exp(math.log(1.0000000116860974e-07) - 4.6051702 * jax.random.uniform(part_splits[4], (2, FW, D), jnp.float32) ** levels(part_splits[4], (2, FW, D), ((1, 8), (2, 2)), -0.2, 0.2)), 9.999999717180685e-10, 1.0000000116860974e-07)
    return {"tokens": tokens, "hidden_grad": hidden_grad, "weights": weights, "first_moment": first_moment, "second_moment": second_moment}


clip_norm = 1.0
beta_one = 0.9
beta_two = 0.95
step_count = 10.0
adam_eps = 1e-08
decay_rate = 0.1

def swiglu_terms(tokens, incoming_grad, gate_rows, up_rows):
    contract = (((1,), (1,)), ((), ()))
    gate = lax.dot_general(tokens, gate_rows, contract, preferred_element_type=jnp.float32)
    upper = lax.dot_general(tokens, up_rows, contract, preferred_element_type=jnp.float32)
    sigma = jax.nn.sigmoid(gate)
    activated = gate * sigma
    hidden = (activated * upper).astype(jnp.bfloat16)
    incoming = incoming_grad.astype(jnp.float32)
    gate_grad = (incoming * upper * sigma * (1.0 + gate * (1.0 - sigma))).astype(jnp.bfloat16)
    up_grad = (incoming * activated).astype(jnp.bfloat16)
    return (hidden, gate_grad, up_grad)

def adam_update(gradient, first_moment, second_moment, weights, norm_sq):
    clip_scale = jnp.minimum(1.0, clip_norm / jnp.sqrt(norm_sq))
    clipped = gradient * clip_scale
    first = beta_one * first_moment + (1.0 - beta_one) * clipped
    second = beta_two * second_moment + (1.0 - beta_two) * clipped * clipped
    first_hat = first / (1.0 - beta_one ** step_count)
    second_hat = second / (1.0 - beta_two ** step_count)
    return first_hat / (jnp.sqrt(second_hat) + adam_eps) + decay_rate * weights.astype(jnp.float32)

def reference(tokens, hidden_grad, weights, first_moment, second_moment):
    block_rows = N_REP * TOK_DEV
    token_blocks = tokens.reshape(N_BLK, block_rows, D)
    grad_blocks = hidden_grad.reshape(N_BLK, block_rows, WINDOW, PANEL)
    panels = weights.reshape(2, N_BLK, PANEL, D)
    contract = (((0,), (0,)), ((), ()))

    def visit(gradient, inputs):
        block_index, block_tokens, block_grad = inputs
        slot_outs = []
        for slot in range(WINDOW):
            owner = jnp.mod(block_index - slot, N_BLK).astype(jnp.int32)
            panel_rows = lax.dynamic_index_in_dim(panels, owner, 1, keepdims=False)
            hidden, gate_grad, up_grad = swiglu_terms(block_tokens, block_grad[:, slot, :], panel_rows[0], panel_rows[1])
            gate_term = lax.dot_general(gate_grad, block_tokens, contract, preferred_element_type=jnp.float32)
            up_term = lax.dot_general(up_grad, block_tokens, contract, preferred_element_type=jnp.float32)
            current = lax.dynamic_index_in_dim(gradient, owner, 1, keepdims=False)
            updated = current + jnp.stack([gate_term, up_term], axis=0)
            gradient = lax.dynamic_update_index_in_dim(gradient, updated, owner, 1)
            slot_outs.append(hidden)
        return (gradient, jnp.stack(slot_outs, axis=1))
    initial = jnp.zeros((2, N_BLK, PANEL, D), jnp.float32)
    block_ids = jnp.arange(N_BLK, dtype=jnp.int32)
    gradient, hidden = lax.scan(visit, initial, (block_ids, token_blocks, grad_blocks))
    hidden = hidden.reshape(TOKENS, WINDOW * PANEL)
    gradient = gradient.reshape(2, FW, D)
    norm_sq = jnp.sum(gradient * gradient)
    adam_step = adam_update(gradient, first_moment, second_moment, weights, norm_sq)
    return (hidden, adam_step)
```

```python
import jax
import jax.numpy as jnp
from jax import lax
from jax.experimental import pallas as pl
from jax.experimental.pallas import tpu as pltpu
from jax.sharding import PartitionSpec as P

clip_norm = 1.0
beta_one = 0.9
beta_two = 0.95
step_count = 10.0
adam_eps = 1e-08
decay_rate = 0.1


def shifted(value, axis, by):
    devices = lax.axis_size(axis)
    return lax.ppermute(value, axis, [(i, (i + by) % devices) for i in range(devices)])


def swiglu_terms(tokens, incoming_grad, gate_rows, up_rows):
    contract = (((1,), (1,)), ((), ()))
    gate = lax.dot_general(tokens, gate_rows, contract, preferred_element_type=jnp.float32)
    upper = lax.dot_general(tokens, up_rows, contract, preferred_element_type=jnp.float32)
    sigma = jax.nn.sigmoid(gate)
    activated = gate * sigma
    hidden = (activated * upper).astype(jnp.bfloat16)
    incoming = incoming_grad.astype(jnp.float32)
    gate_grad = (incoming * upper * sigma * (1.0 + gate * (1.0 - sigma))).astype(jnp.bfloat16)
    up_grad = (incoming * activated).astype(jnp.bfloat16)
    return (hidden, gate_grad, up_grad)


def adam_update(gradient, first_moment, second_moment, weights, norm_sq):
    clip_scale = jnp.minimum(1.0, clip_norm / jnp.sqrt(norm_sq))
    clipped = gradient * clip_scale
    first = beta_one * first_moment + (1.0 - beta_one) * clipped
    second = beta_two * second_moment + (1.0 - beta_two) * clipped * clipped
    first_hat = first / (1.0 - beta_one**step_count)
    second_hat = second / (1.0 - beta_two**step_count)
    return first_hat / (jnp.sqrt(second_hat) + adam_eps) + decay_rate * weights.astype(jnp.float32)


def on_device(tokens, hidden_grad, weights, first_moment, second_moment):
    unit_count = weights.shape[1]
    token_count = tokens.shape[0]
    slot_count = hidden_grad.shape[1] // unit_count
    own_full = lax.all_gather(weights, "rep", axis=2, tiled=True)
    slot_grads = jnp.swapaxes(hidden_grad.reshape(token_count, slot_count, unit_count), 0, 1)
    contract = (((1,), (0,)), ((), ()))

    def grad_term(gate_grad, up_grad):
        paired = jnp.stack([gate_grad, up_grad], axis=0)
        return lax.dot_general(paired, tokens, contract, preferred_element_type=jnp.float32)

    zero_sums = jnp.zeros((2, unit_count, tokens.shape[1]), jnp.float32)

    def visit(panel_rows, slot_grad):
        hidden, gate_grad, up_grad = swiglu_terms(tokens, slot_grad, panel_rows[0], panel_rows[1])
        arrived = shifted(panel_rows, "blk", 1)
        return (arrived, (hidden, gate_grad, up_grad))

    _, (hidden_slots, gate_slots, up_slots) = lax.scan(visit, own_full, slot_grads)

    def collect(running, grads_pair):
        arrived = shifted(running, "blk", -1)
        return (arrived + grad_term(grads_pair[0], grads_pair[1]), None)

    owned_sums, _ = lax.scan(collect, zero_sums, (gate_slots, up_slots), reverse=True)
    hidden = jnp.swapaxes(hidden_slots, 0, 1).reshape(token_count, slot_count * unit_count)
    gradient = lax.psum_scatter(owned_sums, "rep", scatter_dimension=2, tiled=True)
    norm_sq = lax.psum(jnp.sum(gradient * gradient), ("blk", "rep"))
    update = adam_update(gradient, first_moment, second_moment, weights, norm_sq)
    adam_step = lax.all_gather(update, "rep", axis=2, tiled=True)
    return (hidden, adam_step)


def adam_kernel(norm_ref, *refs):
    own, other, out_ref = refs[:4], refs[4:8], refs[8]
    features = own[0].shape[-1]
    scale = jnp.minimum(1.0, clip_norm / jnp.sqrt(norm_ref[0:1, 0:1]))

    def write(values, first):
        gradient, first_moment, second_moment, weights = (ref[0] for ref in values)
        clipped = gradient * scale
        moment = beta_one * first_moment + (1.0 - beta_one) * clipped
        square = beta_two * second_moment + (1.0 - beta_two) * clipped * clipped
        moment = moment * (1.0 / (1.0 - beta_one**step_count))
        square = square * (1.0 / (1.0 - beta_two**step_count))
        update = moment / (jnp.sqrt(square) + adam_eps) + decay_rate * weights.astype(jnp.float32)
        out_ref[0, :, first : first + features] = update

    rep = lax.axis_index("rep")

    @pl.when(rep == 0)
    def _():
        write(own, 0)
        write(other, features)

    @pl.when(rep != 0)
    def _():
        write(other, 0)
        write(own, features)


def adam_all(norm_sq, own, other):
    pair, units, features = own[0].shape
    tile = min(units, 256)
    block = pl.BlockSpec((1, tile, features), lambda i, j: (i, j, 0))
    return pl.pallas_call(
        adam_kernel,
        grid=(pair, units // tile),
        out_shape=jax.ShapeDtypeStruct((pair, units, 2 * features), jnp.float32),
        in_specs=[pl.BlockSpec((8, 128), lambda i, j: (0, 0))] + [block] * 8,
        out_specs=pl.BlockSpec((1, tile, 2 * features), lambda i, j: (i, j, 0)),
        compiler_params=pltpu.CompilerParams(vmem_limit_bytes=32 * 1024 * 1024),
    )(norm_sq, *own, *other)


def cycle_kernel(
    tokens_hbm, grad_hbm, weights_hbm, hidden_hbm, out_ref, other_ref, norm_ref,
    tok, tok_near, incoming_ref, hid, mine, other, grads_c, grads_o, grads_in, x_out, x_in, z_out, z_in, squares, slots,
    load_sem, hid_sem, ag_recv, inner_send, outer_send, x_send, y_send, y_recv, near_send, near_recv, tok_sem,
    g_send, g_recv, xr_send, xr_recv, zr_send, zr_recv, swap_send, swap_recv, norm_send, norm_recv
):
    devices = lax.axis_size("blk")
    units, features = weights_hbm.shape[1], weights_hbm.shape[2]
    token_count = tok.shape[1]
    part = units // 2
    blk, rep, group = lax.axis_index("blk"), lax.axis_index("rep"), lax.axis_index("groups")
    z, x = blk // 2, blk % 2
    end = 1 - ((z + 1) // 2) % 2
    turn = 1 - 2 * (z // 2)
    is_end, is_mid = end == 1, end == 0
    mesh_ids = pl.DeviceIdType.MESH
    near = {"rep": 1 - rep}
    across = {"groups": 1 - group}
    beside = {"blk": 2 * z + 1 - x}
    inner = {"blk": 2 * (z + turn) + x}
    outer_z = z - turn * (1 - end)
    outer = {"blk": 2 * outer_z + x}
    third_z = z + turn * (4 * end - 1)

    def panel(visit, col):
        at = z + turn * visit if visit < 3 else third_z
        return 2 * at + (x if col == 0 else 1 - x)

    row_at = [pl.multiple_of(group * part, part), pl.multiple_of((1 - group) * part, part)]
    rows_of = [pl.ds(at, part) for at in row_at]
    own_at = pl.multiple_of(rep * features, features)
    other_at = pl.multiple_of((1 - rep) * features, features)
    own_panel = blk

    loads = [
        pltpu.make_async_copy(weights_hbm, mine.at[own_panel], load_sem.at[0]),
        pltpu.make_async_copy(tokens_hbm.at[:, pl.ds(own_at, features)], tok.at[0], load_sem.at[1]),
        pltpu.make_async_copy(tokens_hbm.at[:, pl.ds(other_at, features)], tok.at[1], load_sem.at[2]),
        pltpu.make_async_copy(grad_hbm, incoming_ref, load_sem.at[3]),
    ]
    for copy in loads:
        copy.start()

    members = 2 * devices
    me = blk * 2 + rep

    def member(by):
        peer = (me + by) % members
        return {"blk": peer // 2, "rep": peer % 2}

    barrier = pltpu.get_barrier_semaphore()
    for by in range(1, members):
        pl.semaphore_signal(barrier, inc=1, device_id=member(by), device_id_type=mesh_ids)
    pl.semaphore_signal(barrier, inc=1, device_id=across, device_id_type=mesh_ids)
    pl.semaphore_wait(barrier, members)

    started, started_mid = [], []

    def send(source, target, send_sem, recv_sem, peer, keep=started):
        copy = pltpu.make_async_remote_copy(
            src_ref=source, dst_ref=target, send_sem=send_sem, recv_sem=recv_sem, device_id=peer, device_id_type=mesh_ids
        )
        copy.start()
        if keep is not None:
            keep.append(copy)
        return copy

    def arrive(target, sem, peer):
        pltpu.make_async_remote_copy(
            src_ref=target, dst_ref=target, send_sem=sem, recv_sem=sem, device_id=peer, device_id_type=mesh_ids
        ).wait_recv()

    def piece(q, half, which):
        return mine.at[q, which, rows_of[half]]

    def to_inner(q, which, keep=started, source=None):
        source = piece(q, 0, which) if source is None else source
        send(source, piece(q, 0, which), inner_send.at[q, which], ag_recv.at[q, which], inner, keep)

    def to_outer(visit, col, which, source=None):
        q = panel(visit, col)
        source = piece(q, 0, which) if source is None else source
        send(source, piece(q, 0, which), outer_send.at[q, which], ag_recv.at[q, which], outer, None)
        started_mid.append((outer_send, visit, col, which))

    def departed(ref, sem):
        pltpu.make_async_remote_copy(
            src_ref=ref, dst_ref=ref, send_sem=sem, recv_sem=sem, device_id=inner, device_id_type=mesh_ids
        ).wait_send()

    def wait_piece(q, which):
        arrive(piece(q, 0, which), ag_recv.at[q, which], inner)

    def y_out(visit, col, which):
        q = panel(visit, col)
        send(piece(q, 0, which), piece(q, 0, which), y_send.at[q, which], y_recv.at[q, which], across)

    def near_out(visit, col, half):
        q = panel(visit, col)
        if half == 1:
            for which in range(2):
                arrive(piece(q, 1, which), y_recv.at[q, which], across)
        send(
            mine.at[q, :, rows_of[half]], other.at[q, :, rows_of[half]], near_send.at[q, half], near_recv.at[q, half], near
        )

    def from_x(which):
        q = panel(0, 1)
        wait_piece(q, which)
        to_inner(q, which)

        @pl.when(is_mid)
        def _():
            to_outer(0, 1, which)

        y_out(0, 1, which)

    def from_inner(visit, col, which):
        q = panel(visit, col)
        if visit < 3:
            wait_piece(q, which)

            @pl.when(is_mid)
            def _():
                to_outer(visit, col, which)
        else:

            @pl.when(is_end)
            def _():
                wait_piece(q, which)

    def from_outer(col, which):
        @pl.when(is_mid)
        def _():
            q = panel(3, col)
            wait_piece(q, which)
            to_inner(q, which, None)

        started_mid.append((inner_send, 3, col, which))

    tile = min(token_count, 256)
    across_features = (((1,), (1,)), ((), ()))
    across_tokens = (((0,), (0,)), ((), ()))
    hid_copies, o_sends, x_sends = [], [], []

    def forward(visit, col, half):
        q = panel(visit, col)
        arrive(other.at[q, :, rows_of[half]], near_recv.at[q, half], near)
        slot = (blk - q + devices) % devices
        columns = pl.ds(pl.multiple_of(slot * units + row_at[half], 128), part)
        if len(hid_copies) >= 2:
            hid_copies[-2].wait()
        stage = hid.at[len(hid_copies) % 2]
        if col == 0:
            grads = grads_c.at[visit, half]
        else:
            if len(o_sends) >= 2:
                o_sends[-2].wait_send()
            grads = grads_o.at[len(o_sends) % 2]

        @pl.loop(0, token_count // tile)
        def _(t):
            rows = pl.ds(pl.multiple_of(t * tile, tile), tile)
            own_tokens, other_tokens = tok[0, rows, :], tok[1, rows, :]

            def product(which):
                return lax.dot_general(
                    own_tokens, mine[q, which, rows_of[half], :], across_features, preferred_element_type=jnp.float32
                ) + lax.dot_general(
                    other_tokens, other[q, which, rows_of[half], :], across_features, preferred_element_type=jnp.float32
                )

            gate, upper = product(0), product(1)
            incoming = incoming_ref[rows, columns].astype(jnp.float32)
            sigma = jax.nn.sigmoid(gate)
            activated = gate * sigma
            stage[rows, :] = (activated * upper).astype(jnp.bfloat16)
            grads[0, rows, :] = (incoming * upper * sigma * (1.0 + gate * (1.0 - sigma))).astype(jnp.bfloat16)
            grads[1, rows, :] = (incoming * activated).astype(jnp.bfloat16)

        copy = pltpu.make_async_copy(stage, hidden_hbm.at[:, columns], hid_sem.at[len(hid_copies) % 2])
        copy.start()
        hid_copies.append(copy)
        copy = send(
            grads, grads_in.at[visit, col, half], g_send.at[visit, col, half], g_recv.at[visit, col, half], near,
            started if col == 0 else None,
        )
        if col == 1:
            o_sends.append(copy)

    def gradient_term(grads, got, which):
        return lax.dot_general(
            grads[which], tok[0], across_tokens, preferred_element_type=jnp.float32
        ) + lax.dot_general(got[which], tok_near[...], across_tokens, preferred_element_type=jnp.float32)

    def give(visit, half, slot):
        got = grads_in.at[visit, 1, half]
        arrive(got, g_recv.at[visit, 1, half], near)
        order = len(x_sends) // 2
        if order >= 4:
            for copy in x_sends[2 * order - 8 : 2 * order - 6]:
                copy.wait_send()
        for which in range(2):
            target = x_out.at[order % 4, which]
            target[...] = gradient_term(grads_o.at[slot], got, which).astype(jnp.bfloat16)
            x_sends.append(
                send(
                    target, x_in.at[visit, half, which], xr_send.at[visit, half, which], xr_recv.at[visit, half, which],
                    beside, None,
                )
            )

    def arrived_z(slot, half, which):
        arrive(z_in.at[slot, half, which], zr_recv.at[slot, half, which], inner)

    def collect(visit, half, role):
        def run():
            got = grads_in.at[visit, 0, half]
            arrive(got, g_recv.at[visit, 0, half], near)
            to = visit - 1 if role == "end" else 3 + visit % 2
            peer = outer if role == "mid" and visit == 3 else inner
            for which in range(2):
                arrive(x_in.at[visit, half, which], xr_recv.at[visit, half, which], beside)
                if role == "mid":
                    arrived_z(visit, half, which)
                total = gradient_term(grads_c.at[visit, half], got, which)
                total = total + x_in[visit, half, which].astype(jnp.float32)
                if role == "mid":
                    total = total + z_in[visit, half, which].astype(jnp.float32)
                target = z_out.at[visit - 1, half, which]
                target[...] = total.astype(jnp.bfloat16)
                send(
                    target, z_in.at[to, half, which], zr_send.at[visit - 1, half, which], zr_recv.at[to, half, which],
                    peer, None,
                )

        pl.when(is_end if role == "end" else is_mid)(run)

    def finish(half):
        got = grads_in.at[0, 0, half]
        arrive(got, g_recv.at[0, 0, half], near)
        for which in range(2):
            arrive(x_in.at[0, half, which], xr_recv.at[0, half, which], beside)
            arrived_z(4, half, which)
            total = gradient_term(grads_c.at[0, half], got, which)
            total = total + x_in[0, half, which].astype(jnp.float32) + z_in[4, half, which].astype(jnp.float32)
            out_ref[which, rows_of[half], :] = total

            @pl.when(is_mid)
            def _():
                arrived_z(0, half, which)
                out_ref[which, rows_of[half], :] += z_in[0, half, which].astype(jnp.float32)

            total = out_ref[which, rows_of[half], :]
            folded = jnp.sum((total * total).reshape(part // 8, 8, features), axis=0)
            for lane in range(0, features, 128):
                squares[...] += folded[:, lane : lane + 128]
            send(
                out_ref.at[which, rows_of[half]], other_ref.at[which, rows_of[half]], swap_send.at[half, which],
                swap_recv.at[half, which], near,
            )

    for which in range(2):
        source = weights_hbm.at[which, rows_of[0]]
        send(source, piece(own_panel, 0, which), x_send.at[which], ag_recv.at[own_panel, which], beside)
        to_inner(own_panel, which, source=source)

        @pl.when(is_mid)
        def _():
            to_outer(0, 0, which, source=source)

    for half in range(2):
        send(
            weights_hbm.at[:, rows_of[half]], other.at[own_panel, :, rows_of[half]], near_send.at[own_panel, half],
            near_recv.at[own_panel, half], near,
        )
    loads[1].wait()
    loads[2].wait()
    send(tok.at[1], tok_near, tok_sem.at[0], tok_sem.at[1], near)
    loads[0].wait()
    loads[3].wait()
    squares[...] = jnp.zeros_like(squares)
    forward(0, 0, 0)
    forward(0, 0, 1)
    arrive(tok_near, tok_sem.at[1], near)

    from_x(0)
    from_inner(1, 0, 0)
    from_outer(0, 0)
    from_x(1)
    from_inner(1, 0, 1)
    from_outer(0, 1)
    near_out(0, 1, 0)
    forward(0, 1, 0)
    give(0, 0, 0)
    from_inner(1, 1, 0)
    from_outer(1, 0)
    y_out(1, 1, 0)
    near_out(0, 1, 1)
    from_inner(1, 1, 1)
    from_outer(1, 1)
    y_out(1, 1, 1)
    near_out(1, 1, 0)
    forward(1, 1, 0)
    give(1, 0, 1)
    y_out(1, 0, 0)
    y_out(1, 0, 1)
    near_out(1, 0, 0)
    forward(1, 0, 0)
    from_inner(2, 0, 0)
    near_out(1, 1, 1)
    forward(1, 1, 1)
    give(1, 1, 0)
    from_inner(2, 0, 1)
    from_inner(2, 1, 0)
    y_out(2, 1, 0)
    near_out(1, 0, 1)
    forward(1, 0, 1)
    collect(1, 0, "end")
    from_inner(2, 1, 1)
    y_out(2, 1, 1)
    near_out(2, 1, 0)
    forward(2, 1, 0)
    give(2, 0, 1)
    y_out(2, 0, 0)
    y_out(2, 0, 1)
    near_out(2, 0, 0)
    forward(2, 0, 0)
    from_inner(3, 0, 0)
    near_out(2, 1, 1)
    forward(2, 1, 1)
    give(2, 1, 0)
    collect(1, 1, "end")
    from_inner(3, 0, 1)
    from_inner(3, 1, 0)
    y_out(3, 1, 0)
    near_out(2, 0, 1)
    forward(2, 0, 1)
    collect(2, 0, "end")
    from_inner(3, 1, 1)
    y_out(3, 1, 1)
    near_out(3, 1, 0)
    forward(3, 1, 0)
    give(3, 0, 1)
    y_out(3, 0, 0)
    y_out(3, 0, 1)
    near_out(3, 0, 0)
    forward(3, 0, 0)
    near_out(3, 1, 1)
    forward(3, 1, 1)
    give(3, 1, 0)
    forward(0, 1, 1)
    give(0, 1, 1)
    collect(2, 1, "end")
    collect(1, 0, "mid")
    near_out(3, 0, 1)
    forward(3, 0, 1)
    collect(3, 0, "end")
    collect(1, 1, "mid")
    collect(3, 1, "end")
    collect(2, 0, "mid")
    collect(2, 1, "mid")
    collect(3, 0, "mid")
    collect(3, 1, "mid")
    finish(0)
    finish(1)

    slots[me] = squares[...]
    copies = []
    for by in range(1, members):
        copies.append(
            send(squares, slots.at[me], norm_send.at[by], norm_recv.at[by], member(by), None)
        )
    for copy in copies:
        copy.wait()
    total = slots[0]
    for i in range(1, members):
        total = total + slots[i]
    norm_ref[...] = jnp.full(norm_ref.shape, jnp.sum(total), jnp.float32)
    for copy in started + o_sends[-2:] + x_sends[-8:]:
        copy.wait_send()
    for visit in range(3):
        for half in range(2):
            for which in range(2):
                departed(z_out.at[visit, half, which], zr_send.at[visit, half, which])

    @pl.when(is_mid)
    def _():
        for sems, visit, col, which in started_mid:
            q = panel(visit, col)
            departed(piece(q, 0, which), sems.at[q, which])

    for copy in hid_copies[-2:]:
        copy.wait()
    for half in range(2):
        for which in range(2):
            arrive(other_ref.at[which, rows_of[half]], swap_recv.at[half, which], near)


def cycle_all(tokens, hidden_grad, weights):
    devices = lax.axis_size("blk")
    units, features = weights.shape[1], weights.shape[2]
    token_count = tokens.shape[0]
    part = units // 2
    bf16, f32 = jnp.bfloat16, jnp.float32
    vmem, anywhere = pl.BlockSpec(memory_space=pltpu.VMEM), pl.BlockSpec(memory_space=pl.ANY)
    dma = pltpu.SemaphoreType.DMA
    grads = (2, token_count, part)
    sums = (2, part, features)
    return pl.pallas_call(
        cycle_kernel,
        out_shape=(
            jax.ShapeDtypeStruct(hidden_grad.shape, bf16),
            jax.ShapeDtypeStruct((2, units, features), f32),
            jax.ShapeDtypeStruct((2, units, features), f32),
            jax.ShapeDtypeStruct((8, 128), f32),
        ),
        in_specs=[anywhere] * 3,
        out_specs=(anywhere, vmem, anywhere, vmem),
        scratch_shapes=[
            pltpu.VMEM((2, token_count, features), bf16),
            pltpu.VMEM((token_count, features), bf16),
            pltpu.VMEM(hidden_grad.shape, bf16),
            pltpu.VMEM((2, token_count, part), bf16),
            pltpu.VMEM((devices, 2, units, features), bf16),
            pltpu.VMEM((devices, 2, units, features), bf16),
            pltpu.VMEM((4, 2) + grads, bf16),
            pltpu.VMEM((2,) + grads, bf16),
            pltpu.VMEM((4, 2, 2) + grads, bf16),
            pltpu.VMEM((4,) + sums, bf16),
            pltpu.VMEM((4, 2) + sums, bf16),
            pltpu.VMEM((3, 2) + sums, bf16),
            pltpu.VMEM((5, 2) + sums, bf16),
            pltpu.VMEM((8, 128), f32),
            pltpu.VMEM((2 * devices, 8, 128), f32),
            dma((4,)), dma((2,)),
            dma((devices, 2)), dma((devices, 2)), dma((devices, 2)), dma((2,)), dma((devices, 2)), dma((devices, 2)),
            dma((devices, 2)), dma((devices, 2)), dma((2,)),
            dma((4, 2, 2)), dma((4, 2, 2)), dma((4, 2, 2)), dma((4, 2, 2)), dma((3, 2, 2)), dma((5, 2, 2)),
            dma((2, 2)), dma((2, 2)), dma((2 * devices,)), dma((2 * devices,)),
        ],
        compiler_params=pltpu.CompilerParams(
            collective_id=1, has_side_effects=True, vmem_limit_bytes=58 * 1024 * 1024
        ),
    )(tokens, hidden_grad, weights)


def on_ring(tokens, hidden_grad, weights, first_moment, second_moment):
    def partner(value):
        return lax.ppermute(value, "rep", [(0, 1), (1, 0)])

    hidden, gradient, other_gradient, norm_sq = cycle_all(tokens, hidden_grad, weights)
    own = (first_moment, second_moment, weights)
    other = tuple(partner(value) for value in own)
    update = adam_all(norm_sq, (gradient,) + own, (other_gradient,) + other)
    return (hidden, update)


def solution(mesh):
    placed = (
        P(("groups", "blk", "rep"), None),
        P(("groups", "blk", "rep"), None),
        P(None, "blk", "rep"),
        P(None, ("groups", "blk"), "rep"),
        P(None, ("groups", "blk"), "rep"),
    )
    devices = mesh.shape["blk"]

    def program(tokens, hidden_grad, weights, first_moment, second_moment):
        slots = hidden_grad.shape[1] * devices // weights.shape[1]
        whole_cycle = slots == devices and devices == 8 and mesh.shape["rep"] == 2 and mesh.shape["groups"] == 2
        step = jax.shard_map(
            on_ring if whole_cycle else on_device,
            mesh=mesh,
            in_specs=placed,
            out_specs=(P(("groups", "blk", "rep"), None), P(None, ("groups", "blk"), None)),
            check_vma=False,
        )
        return step(tokens, hidden_grad, weights, first_moment, second_moment)

    return program
```

```python
import jax
import jax.numpy as jnp
from jax import lax
from jax.experimental import pallas as pl
from jax.experimental.pallas import tpu as pltpu
from jax.sharding import PartitionSpec as P

clip_norm = 1.0
beta_one = 0.9
beta_two = 0.95
step_count = 10.0
adam_eps = 1e-08
decay_rate = 0.1
PIECES = 4


def shifted(value, axis, by):
    devices = lax.axis_size(axis)
    return lax.ppermute(value, axis, [(i, (i + by) % devices) for i in range(devices)])


def swiglu_terms(tokens, incoming_grad, gate_rows, up_rows):
    contract = (((1,), (1,)), ((), ()))
    gate = lax.dot_general(tokens, gate_rows, contract, preferred_element_type=jnp.float32)
    upper = lax.dot_general(tokens, up_rows, contract, preferred_element_type=jnp.float32)
    sigma = jax.nn.sigmoid(gate)
    activated = gate * sigma
    hidden = (activated * upper).astype(jnp.bfloat16)
    incoming = incoming_grad.astype(jnp.float32)
    gate_grad = (incoming * upper * sigma * (1.0 + gate * (1.0 - sigma))).astype(jnp.bfloat16)
    up_grad = (incoming * activated).astype(jnp.bfloat16)
    return (hidden, gate_grad, up_grad)


def adam_update(gradient, first_moment, second_moment, weights, norm_sq):
    clip_scale = jnp.minimum(1.0, clip_norm / jnp.sqrt(norm_sq))
    clipped = gradient * clip_scale
    first = beta_one * first_moment + (1.0 - beta_one) * clipped
    second = beta_two * second_moment + (1.0 - beta_two) * clipped * clipped
    first_hat = first / (1.0 - beta_one**step_count)
    second_hat = second / (1.0 - beta_two**step_count)
    return first_hat / (jnp.sqrt(second_hat) + adam_eps) + decay_rate * weights.astype(jnp.float32)


def on_device(tokens, hidden_grad, weights, first_moment, second_moment):
    unit_count = weights.shape[1]
    token_count = tokens.shape[0]
    slot_count = hidden_grad.shape[1] // unit_count
    own_full = lax.all_gather(weights, "rep", axis=2, tiled=True)
    slot_grads = jnp.swapaxes(hidden_grad.reshape(token_count, slot_count, unit_count), 0, 1)
    contract = (((1,), (0,)), ((), ()))

    def grad_term(gate_grad, up_grad):
        paired = jnp.stack([gate_grad, up_grad], axis=0)
        return lax.dot_general(paired, tokens, contract, preferred_element_type=jnp.float32)

    zero_sums = jnp.zeros((2, unit_count, tokens.shape[1]), jnp.float32)

    def visit(panel_rows, slot_grad):
        hidden, gate_grad, up_grad = swiglu_terms(tokens, slot_grad, panel_rows[0], panel_rows[1])
        arrived = shifted(panel_rows, "blk", 1)
        return (arrived, (hidden, gate_grad, up_grad))

    _, (hidden_slots, gate_slots, up_slots) = lax.scan(visit, own_full, slot_grads)

    def collect(running, grads_pair):
        arrived = shifted(running, "blk", -1)
        return (arrived + grad_term(grads_pair[0], grads_pair[1]), None)

    owned_sums, _ = lax.scan(collect, zero_sums, (gate_slots, up_slots), reverse=True)
    hidden = jnp.swapaxes(hidden_slots, 0, 1).reshape(token_count, slot_count * unit_count)
    gradient = lax.psum_scatter(owned_sums, "rep", scatter_dimension=2, tiled=True)
    norm_sq = lax.psum(jnp.sum(gradient * gradient), ("blk", "rep"))
    update = adam_update(gradient, first_moment, second_moment, weights, norm_sq)
    adam_step = lax.all_gather(update, "rep", axis=2, tiled=True)
    return (hidden, adam_step)


def adam_kernel(norm_ref, *refs):
    own, other, out_ref = refs[:4], refs[4:8], refs[8]
    features = own[0].shape[-1]
    scale = jnp.minimum(1.0, clip_norm / jnp.sqrt(norm_ref[0:1, 0:1]))

    def write(values, first):
        gradient, first_moment, second_moment, weights = (ref[0] for ref in values)
        clipped = gradient * scale
        moment = beta_one * first_moment + (1.0 - beta_one) * clipped
        square = beta_two * second_moment + (1.0 - beta_two) * clipped * clipped
        moment = moment * (1.0 / (1.0 - beta_one**step_count))
        square = square * (1.0 / (1.0 - beta_two**step_count))
        update = moment / (jnp.sqrt(square) + adam_eps) + decay_rate * weights.astype(jnp.float32)
        out_ref[0, :, first : first + features] = update

    rep = lax.axis_index("rep")

    @pl.when(rep == 0)
    def _():
        write(own, 0)
        write(other, features)

    @pl.when(rep != 0)
    def _():
        write(other, 0)
        write(own, features)


def adam_all(norm_sq, own, other):
    pair, units, features = own[0].shape
    tile = min(units, 256)
    block = pl.BlockSpec((1, tile, features), lambda i, j: (i, j, 0))
    return pl.pallas_call(
        adam_kernel,
        grid=(pair, units // tile),
        out_shape=jax.ShapeDtypeStruct((pair, units, 2 * features), jnp.float32),
        in_specs=[pl.BlockSpec((8, 128), lambda i, j: (0, 0))] + [block] * 8,
        out_specs=pl.BlockSpec((1, tile, 2 * features), lambda i, j: (i, j, 0)),
        compiler_params=pltpu.CompilerParams(vmem_limit_bytes=32 * 1024 * 1024),
    )(norm_sq, *own, *other)


def cycle_kernel(
    tokens_hbm, grad_hbm, weights_hbm, hidden_hbm, out_ref, other_ref, norm_ref,
    tok, tok_near, incoming_ref, hid, mine, other, grads_out, grads_in, x_out, x_in, z_in, sums, squares, slots,
    load_sem, hid_sem, ag_recv, inner_send, outer_send, x_send, y_send, y_recv, near_send, near_recv, tok_sem,
    g_send, g_recv, xr_send, xr_recv, zr_send, zr_recv, swap_send, swap_recv, norm_send, norm_recv
):
    devices = lax.axis_size("blk")
    units, features = weights_hbm.shape[1], weights_hbm.shape[2]
    token_count = tok.shape[1]
    part = units // 2
    blk, rep, group = lax.axis_index("blk"), lax.axis_index("rep"), lax.axis_index("groups")
    z, x = blk // 2, blk % 2
    end = 1 - ((z + 1) // 2) % 2
    turn = 1 - 2 * (z // 2)
    is_end, is_mid = end == 1, end == 0
    mesh_ids = pl.DeviceIdType.MESH
    near = {"rep": 1 - rep}
    across = {"groups": 1 - group}
    beside = {"blk": 2 * z + 1 - x}
    inner = {"blk": 2 * (z + turn) + x}
    outer_z = z - turn * (1 - end)
    outer = {"blk": 2 * outer_z + x}
    third_z = z + turn * (4 * end - 1)

    def panel(visit, col):
        at = z + turn * visit if visit < 3 else third_z
        return 2 * at + (x if col == 0 else 1 - x)

    row_at = [pl.multiple_of(group * part, part), pl.multiple_of((1 - group) * part, part)]
    rows_of = [pl.ds(at, part) for at in row_at]
    own_at = pl.multiple_of(rep * features, features)
    other_at = pl.multiple_of((1 - rep) * features, features)
    own_panel = blk

    loads = [
        pltpu.make_async_copy(weights_hbm, mine.at[own_panel], load_sem.at[0]),
        pltpu.make_async_copy(tokens_hbm.at[:, pl.ds(own_at, features)], tok.at[0], load_sem.at[1]),
        pltpu.make_async_copy(tokens_hbm.at[:, pl.ds(other_at, features)], tok.at[1], load_sem.at[2]),
        pltpu.make_async_copy(grad_hbm, incoming_ref, load_sem.at[3]),
    ]
    for copy in loads:
        copy.start()

    members = 2 * devices
    me = blk * 2 + rep

    def member(by):
        peer = (me + by) % members
        return {"blk": peer // 2, "rep": peer % 2}

    barrier = pltpu.get_barrier_semaphore()
    for by in range(1, members):
        pl.semaphore_signal(barrier, inc=1, device_id=member(by), device_id_type=mesh_ids)
    pl.semaphore_signal(barrier, inc=1, device_id=across, device_id_type=mesh_ids)
    pl.semaphore_wait(barrier, members)

    started, started_mid = [], []

    def send(source, target, send_sem, recv_sem, peer, keep=started):
        copy = pltpu.make_async_remote_copy(
            src_ref=source, dst_ref=target, send_sem=send_sem, recv_sem=recv_sem, device_id=peer, device_id_type=mesh_ids
        )
        copy.start()
        if keep is not None:
            keep.append(copy)
        return copy

    def arrive(target, sem, peer):
        pltpu.make_async_remote_copy(
            src_ref=target, dst_ref=target, send_sem=sem, recv_sem=sem, device_id=peer, device_id_type=mesh_ids
        ).wait_recv()

    def piece(q, half, which):
        return mine.at[q, which, rows_of[half]]

    def to_inner(q, which, keep=started, source=None):
        source = piece(q, 0, which) if source is None else source
        send(source, piece(q, 0, which), inner_send.at[q, which], ag_recv.at[q, which], inner, keep)

    def to_outer(visit, col, which, source=None):
        q = panel(visit, col)
        source = piece(q, 0, which) if source is None else source
        send(source, piece(q, 0, which), outer_send.at[q, which], ag_recv.at[q, which], outer, None)
        started_mid.append((outer_send, visit, col, which))

    def departed(ref, sem):
        pltpu.make_async_remote_copy(
            src_ref=ref, dst_ref=ref, send_sem=sem, recv_sem=sem, device_id=inner, device_id_type=mesh_ids
        ).wait_send()

    def wait_piece(q, which):
        arrive(piece(q, 0, which), ag_recv.at[q, which], inner)

    def y_out(visit, col, which):
        q = panel(visit, col)
        send(piece(q, 0, which), piece(q, 0, which), y_send.at[q, which], y_recv.at[q, which], across)

    def near_out(visit, col, half):
        q = panel(visit, col)
        if half == 1:
            for which in range(2):
                arrive(piece(q, 1, which), y_recv.at[q, which], across)
        send(
            mine.at[q, :, rows_of[half]], other.at[q, :, rows_of[half]], near_send.at[q, half], near_recv.at[q, half], near
        )

    def from_x(which):
        q = panel(0, 1)
        wait_piece(q, which)
        to_inner(q, which)

        @pl.when(is_mid)
        def _():
            to_outer(0, 1, which)

        y_out(0, 1, which)

    def from_inner(visit, col, which):
        q = panel(visit, col)
        if visit < 3:
            wait_piece(q, which)

            @pl.when(is_mid)
            def _():
                to_outer(visit, col, which)
        else:

            @pl.when(is_end)
            def _():
                wait_piece(q, which)

    def from_outer(col, which):
        @pl.when(is_mid)
        def _():
            q = panel(3, col)
            wait_piece(q, which)
            to_inner(q, which, None)

        started_mid.append((inner_send, 3, col, which))

    tile = min(token_count, 256)
    across_features = (((1,), (1,)), ((), ()))
    across_tokens = (((0,), (0,)), ((), ()))
    hid_copies, g_copies, x_copies, ring_at = [], [], [], {}
    ring = grads_out.shape[0]

    def forward(visit, col, half):
        q = panel(visit, col)
        arrive(other.at[q, :, rows_of[half]], near_recv.at[q, half], near)
        slot = (blk - q + devices) % devices
        columns = pl.ds(pl.multiple_of(slot * units + row_at[half], 128), part)
        if len(hid_copies) >= 2:
            hid_copies[-2].wait()
        stage = hid.at[len(hid_copies) % 2]
        if len(g_copies) >= ring:
            g_copies[-ring].wait_send()
        ring_at[visit, col, half] = len(g_copies) % ring
        grads = grads_out.at[len(g_copies) % ring]

        @pl.loop(0, token_count // tile)
        def _(t):
            rows = pl.ds(pl.multiple_of(t * tile, tile), tile)
            own_tokens, other_tokens = tok[0, rows, :], tok[1, rows, :]

            def product(which):
                return lax.dot_general(
                    own_tokens, mine[q, which, rows_of[half], :], across_features, preferred_element_type=jnp.float32
                ) + lax.dot_general(
                    other_tokens, other[q, which, rows_of[half], :], across_features, preferred_element_type=jnp.float32
                )

            gate, upper = product(0), product(1)
            incoming = incoming_ref[rows, columns].astype(jnp.float32)
            sigma = jax.nn.sigmoid(gate)
            activated = gate * sigma
            stage[rows, :] = (activated * upper).astype(jnp.bfloat16)
            grads[0, rows, :] = (incoming * upper * sigma * (1.0 + gate * (1.0 - sigma))).astype(jnp.bfloat16)
            grads[1, rows, :] = (incoming * activated).astype(jnp.bfloat16)

        copy = pltpu.make_async_copy(stage, hidden_hbm.at[:, columns], hid_sem.at[len(hid_copies) % 2])
        copy.start()
        hid_copies.append(copy)
        g_copies.append(
            send(
                grads, grads_in.at[visit, col, half], g_send.at[visit, col, half], g_recv.at[visit, col, half], near, None
            )
        )

    def gradient_term(visit, col, half, which, rows):
        grads = grads_out.at[ring_at[visit, col, half]]
        got = grads_in.at[visit, col, half]
        return lax.dot_general(
            grads[which, :, rows], tok[0], across_tokens, preferred_element_type=jnp.float32
        ) + lax.dot_general(got[which, :, rows], tok_near[...], across_tokens, preferred_element_type=jnp.float32)

    step = part // (PIECES // 2)
    pieces = [(which, pl.ds(first, step)) for which in range(2) for first in range(0, part, step)]

    def give(visit, half):
        got = grads_in.at[visit, 1, half]
        arrive(got, g_recv.at[visit, 1, half], near)
        order = len(x_copies) // PIECES
        for i, (which, rows) in enumerate(pieces):
            target = x_out.at[order, which, rows]
            target[...] = gradient_term(visit, 1, half, which, rows).astype(jnp.bfloat16)
            x_copies.append(
                send(
                    target, x_in.at[visit, half, which, rows], xr_send.at[visit, half, i], xr_recv.at[visit, half, i],
                    beside, None,
                )
            )

    def total_at(visit, half, which, rows):
        if visit == 0:
            first = 0 if rows is None else rows.start
            size = part if rows is None else step
            return out_ref.at[which, pl.ds(pl.multiple_of(row_at[half] + first, step), size)]
        target = sums.at[visit - 1, half, which]
        return target if rows is None else target.at[rows]

    def term(visit, half):
        got = grads_in.at[visit, 0, half]
        arrive(got, g_recv.at[visit, 0, half], near)
        for which in range(2):
            total_at(visit, half, which, None)[...] = gradient_term(visit, 0, half, which, pl.ds(0, part))

    def from_beside(visit, half, i, which, rows):
        arrive(x_in.at[visit, half, which, rows], xr_recv.at[visit, half, i], beside)
        return x_in[visit, half, which, rows, :].astype(jnp.float32)

    def from_line(slot, half, i, which, rows):
        arrive(z_in.at[slot, half, which, rows], zr_recv.at[slot, half, i], inner)
        return z_in[slot, half, which, rows, :].astype(jnp.float32)

    def add_beside(visit, half):
        def run():
            for i, (which, rows) in enumerate(pieces):
                total_at(visit, half, which, rows)[...] += from_beside(visit, half, i, which, rows)

        if visit == 0:
            run()
        else:
            pl.when(is_mid)(run)

    def add_outer(half):
        @pl.when(is_mid)
        def _():
            for i, (which, rows) in enumerate(pieces):
                total_at(0, half, which, rows)[...] += from_line(0, half, i, which, rows)

    def pass_on(visit, half, at_end):
        def run():
            to = visit - 1 if at_end else 3 + visit % 2
            peer = outer if visit == 3 and not at_end else inner
            for i, (which, rows) in enumerate(pieces):
                if at_end:
                    added = from_beside(visit, half, i, which, rows)
                else:
                    added = from_line(visit, half, i, which, rows)
                target = x_in.at[visit, half, which, rows]
                target[...] = (total_at(visit, half, which, rows)[...] + added).astype(jnp.bfloat16)
                send(
                    target, z_in.at[to, half, which, rows], zr_send.at[visit - 1, half, i], zr_recv.at[to, half, i],
                    peer, None,
                )

        pl.when(is_end if at_end else is_mid)(run)

    def finish(half):
        for i, (which, rows) in enumerate(pieces):
            target = total_at(0, half, which, rows)
            total = target[...] + from_line(4, half, i, which, rows)
            target[...] = total
            folded = jnp.sum((total * total).reshape(step // 8, 8, features), axis=0)
            for lane in range(0, features, 128):
                squares[...] += folded[:, lane : lane + 128]
            send(
                target, other_ref.at[which, pl.ds(pl.multiple_of(row_at[half] + rows.start, step), step)],
                swap_send.at[half, i], swap_recv.at[half, i], near,
            )

    for which in range(2):
        source = weights_hbm.at[which, rows_of[0]]
        send(source, piece(own_panel, 0, which), x_send.at[which], ag_recv.at[own_panel, which], beside)
        to_inner(own_panel, which, source=source)

        @pl.when(is_mid)
        def _():
            to_outer(0, 0, which, source=source)

    for half in range(2):
        send(
            weights_hbm.at[:, rows_of[half]], other.at[own_panel, :, rows_of[half]], near_send.at[own_panel, half],
            near_recv.at[own_panel, half], near,
        )
    loads[1].wait()
    loads[2].wait()
    send(tok.at[1], tok_near, tok_sem.at[0], tok_sem.at[1], near)
    loads[0].wait()
    loads[3].wait()
    squares[...] = jnp.zeros_like(squares)
    forward(0, 0, 0)
    forward(0, 0, 1)
    from_x(0)
    arrive(tok_near, tok_sem.at[1], near)
    term(0, 1)
    from_x(1)
    near_out(0, 1, 0)
    forward(0, 1, 0)
    term(0, 0)
    from_inner(1, 1, 0)
    y_out(1, 1, 0)
    give(0, 0)
    from_outer(1, 0)
    from_inner(1, 1, 1)
    from_outer(0, 0)
    from_inner(1, 0, 1)
    near_out(1, 1, 0)
    y_out(1, 1, 1)
    from_outer(1, 1)
    from_inner(1, 0, 0)
    near_out(1, 0, 0)
    from_outer(0, 1)
    forward(1, 1, 0)
    give(1, 0)
    y_out(1, 0, 1)
    from_inner(2, 1, 0)
    near_out(1, 1, 1)
    forward(1, 0, 0)
    y_out(1, 0, 0)
    forward(1, 1, 1)
    give(1, 1)
    term(1, 0)
    from_inner(2, 1, 1)
    near_out(2, 1, 0)
    y_out(2, 1, 1)
    y_out(2, 1, 0)
    pass_on(1, 0, True)
    near_out(1, 0, 1)
    forward(2, 1, 0)
    from_inner(2, 0, 1)
    forward(1, 0, 1)
    from_inner(2, 0, 0)
    near_out(2, 0, 0)
    give(2, 0)
    add_beside(1, 0)
    term(1, 1)
    pass_on(1, 1, True)
    from_inner(3, 1, 0)
    y_out(3, 1, 0)
    forward(2, 0, 0)
    from_inner(3, 1, 1)
    near_out(3, 1, 0)
    y_out(3, 1, 1)
    forward(3, 1, 0)
    term(2, 0)
    give(3, 0)
    pass_on(2, 0, True)
    from_inner(3, 0, 1)
    y_out(3, 0, 1)
    from_inner(3, 0, 0)
    near_out(3, 0, 0)
    y_out(3, 0, 0)
    near_out(2, 1, 1)
    add_outer(0)
    y_out(2, 0, 0)
    near_out(3, 1, 1)
    forward(3, 0, 0)
    forward(3, 1, 1)
    term(3, 0)
    add_outer(1)
    pass_on(3, 0, True)
    give(3, 1)
    add_beside(1, 1)
    y_out(2, 0, 1)
    pass_on(1, 0, False)
    add_beside(3, 0)
    near_out(3, 0, 1)
    forward(2, 1, 1)
    forward(3, 0, 1)
    add_beside(2, 0)
    give(2, 1)
    term(3, 1)
    pass_on(2, 0, False)
    pass_on(3, 1, True)
    near_out(0, 1, 1)
    near_out(2, 0, 1)
    forward(2, 0, 1)
    term(2, 1)
    pass_on(2, 1, True)
    add_beside(2, 1)
    pass_on(2, 1, False)
    pass_on(3, 0, False)
    add_beside(3, 1)
    forward(0, 1, 1)
    add_beside(0, 0)
    give(0, 1)
    pass_on(1, 1, False)
    pass_on(3, 1, False)
    finish(0)
    add_beside(0, 1)
    finish(1)

    slots[me] = squares[...]
    copies = []
    for by in range(1, members):
        copies.append(
            send(squares, slots.at[me], norm_send.at[by], norm_recv.at[by], member(by), None)
        )
    for copy in copies:
        copy.wait()
    total = slots[0]
    for i in range(1, members):
        total = total + slots[i]
    norm_ref[...] = jnp.full(norm_ref.shape, jnp.sum(total), jnp.float32)
    for copy in started + g_copies[-ring:] + x_copies:
        copy.wait_send()
    for visit in range(3):
        for half in range(2):
            for i, (which, rows) in enumerate(pieces):
                departed(x_in.at[visit + 1, half, which, rows], zr_send.at[visit, half, i])

    @pl.when(is_mid)
    def _():
        for sems, visit, col, which in started_mid:
            q = panel(visit, col)
            departed(piece(q, 0, which), sems.at[q, which])

    for copy in hid_copies[-2:]:
        copy.wait()
    for half in range(2):
        for i, (which, rows) in enumerate(pieces):
            arrive(
                other_ref.at[which, pl.ds(pl.multiple_of(row_at[half] + rows.start, step), step)],
                swap_recv.at[half, i], near,
            )


def cycle_all(tokens, hidden_grad, weights):
    devices = lax.axis_size("blk")
    units, features = weights.shape[1], weights.shape[2]
    token_count = tokens.shape[0]
    part = units // 2
    bf16, f32 = jnp.bfloat16, jnp.float32
    vmem, anywhere = pl.BlockSpec(memory_space=pltpu.VMEM), pl.BlockSpec(memory_space=pl.ANY)
    dma = pltpu.SemaphoreType.DMA
    grads = (2, token_count, part)
    sums = (2, part, features)
    return pl.pallas_call(
        cycle_kernel,
        out_shape=(
            jax.ShapeDtypeStruct(hidden_grad.shape, bf16),
            jax.ShapeDtypeStruct((2, units, features), f32),
            jax.ShapeDtypeStruct((2, units, features), f32),
            jax.ShapeDtypeStruct((8, 128), f32),
        ),
        in_specs=[anywhere] * 3,
        out_specs=(anywhere, vmem, anywhere, vmem),
        scratch_shapes=[
            pltpu.VMEM((2, token_count, features), bf16),
            pltpu.VMEM((token_count, features), bf16),
            pltpu.VMEM(hidden_grad.shape, bf16),
            pltpu.VMEM((2, token_count, part), bf16),
            pltpu.VMEM((devices, 2, units, features), bf16),
            pltpu.VMEM((devices, 2, units, features), bf16),
            pltpu.VMEM((4,) + grads, bf16),
            pltpu.VMEM((4, 2, 2) + grads, bf16),
            pltpu.VMEM((8,) + sums, bf16),
            pltpu.VMEM((4, 2) + sums, bf16),
            pltpu.VMEM((5, 2) + sums, bf16),
            pltpu.VMEM((3, 2) + sums, f32),
            pltpu.VMEM((8, 128), f32),
            pltpu.VMEM((2 * devices, 8, 128), f32),
            dma((4,)), dma((2,)),
            dma((devices, 2)), dma((devices, 2)), dma((devices, 2)), dma((2,)), dma((devices, 2)), dma((devices, 2)),
            dma((devices, 2)), dma((devices, 2)), dma((2,)),
            dma((4, 2, 2)), dma((4, 2, 2)), dma((4, 2, PIECES)), dma((4, 2, PIECES)), dma((3, 2, PIECES)),
            dma((5, 2, PIECES)), dma((2, PIECES)), dma((2, PIECES)), dma((2 * devices,)), dma((2 * devices,)),
        ],
        compiler_params=pltpu.CompilerParams(
            collective_id=1, has_side_effects=True, vmem_limit_bytes=58 * 1024 * 1024
        ),
    )(tokens, hidden_grad, weights)


def on_ring(tokens, hidden_grad, weights, first_moment, second_moment):
    def partner(value):
        return lax.ppermute(value, "rep", [(0, 1), (1, 0)])

    hidden, gradient, other_gradient, norm_sq = cycle_all(tokens, hidden_grad, weights)
    own = (first_moment, second_moment, weights)
    other = tuple(partner(value) for value in own)
    update = adam_all(norm_sq, (gradient,) + own, (other_gradient,) + other)
    return (hidden, update)


def solution(mesh):
    placed = (
        P(("groups", "blk", "rep"), None),
        P(("groups", "blk", "rep"), None),
        P(None, "blk", "rep"),
        P(None, ("groups", "blk"), "rep"),
        P(None, ("groups", "blk"), "rep"),
    )
    devices = mesh.shape["blk"]

    def program(tokens, hidden_grad, weights, first_moment, second_moment):
        slots = hidden_grad.shape[1] * devices // weights.shape[1]
        whole_cycle = slots == devices and devices == 8 and mesh.shape["rep"] == 2 and mesh.shape["groups"] == 2
        step = jax.shard_map(
            on_ring if whole_cycle else on_device,
            mesh=mesh,
            in_specs=placed,
            out_specs=(P(("groups", "blk", "rep"), None), P(None, ("groups", "blk"), None)),
            check_vma=False,
        )
        return step(tokens, hidden_grad, weights, first_moment, second_moment)

    return program
```

```python
import jax
import jax.numpy as jnp
from jax import lax
from jax.experimental import pallas as pl
from jax.experimental.pallas import tpu as pltpu
from jax.sharding import PartitionSpec as P

clip_norm = 1.0
beta_one = 0.9
beta_two = 0.95
step_count = 10.0
adam_eps = 1e-08
decay_rate = 0.1
RING = 6


def shifted(value, axis, by):
    devices = lax.axis_size(axis)
    return lax.ppermute(value, axis, [(i, (i + by) % devices) for i in range(devices)])


def swiglu_terms(tokens, incoming_grad, gate_rows, up_rows):
    contract = (((1,), (1,)), ((), ()))
    gate = lax.dot_general(tokens, gate_rows, contract, preferred_element_type=jnp.float32)
    upper = lax.dot_general(tokens, up_rows, contract, preferred_element_type=jnp.float32)
    sigma = jax.nn.sigmoid(gate)
    activated = gate * sigma
    hidden = (activated * upper).astype(jnp.bfloat16)
    incoming = incoming_grad.astype(jnp.float32)
    gate_grad = (incoming * upper * sigma * (1.0 + gate * (1.0 - sigma))).astype(jnp.bfloat16)
    up_grad = (incoming * activated).astype(jnp.bfloat16)
    return (hidden, gate_grad, up_grad)


def adam_update(gradient, first_moment, second_moment, weights, norm_sq):
    clip_scale = jnp.minimum(1.0, clip_norm / jnp.sqrt(norm_sq))
    clipped = gradient * clip_scale
    first = beta_one * first_moment + (1.0 - beta_one) * clipped
    second = beta_two * second_moment + (1.0 - beta_two) * clipped * clipped
    first_hat = first / (1.0 - beta_one**step_count)
    second_hat = second / (1.0 - beta_two**step_count)
    return first_hat / (jnp.sqrt(second_hat) + adam_eps) + decay_rate * weights.astype(jnp.float32)


def on_device(tokens, hidden_grad, weights, first_moment, second_moment):
    unit_count = weights.shape[1]
    token_count = tokens.shape[0]
    slot_count = hidden_grad.shape[1] // unit_count
    own_full = lax.all_gather(weights, "rep", axis=2, tiled=True)
    slot_grads = jnp.swapaxes(hidden_grad.reshape(token_count, slot_count, unit_count), 0, 1)
    contract = (((1,), (0,)), ((), ()))

    def grad_term(gate_grad, up_grad):
        paired = jnp.stack([gate_grad, up_grad], axis=0)
        return lax.dot_general(paired, tokens, contract, preferred_element_type=jnp.float32)

    zero_sums = jnp.zeros((2, unit_count, tokens.shape[1]), jnp.float32)

    def visit(panel_rows, slot_grad):
        hidden, gate_grad, up_grad = swiglu_terms(tokens, slot_grad, panel_rows[0], panel_rows[1])
        arrived = shifted(panel_rows, "blk", 1)
        return (arrived, (hidden, gate_grad, up_grad))

    _, (hidden_slots, gate_slots, up_slots) = lax.scan(visit, own_full, slot_grads)

    def collect(running, grads_pair):
        arrived = shifted(running, "blk", -1)
        return (arrived + grad_term(grads_pair[0], grads_pair[1]), None)

    owned_sums, _ = lax.scan(collect, zero_sums, (gate_slots, up_slots), reverse=True)
    hidden = jnp.swapaxes(hidden_slots, 0, 1).reshape(token_count, slot_count * unit_count)
    gradient = lax.psum_scatter(owned_sums, "rep", scatter_dimension=2, tiled=True)
    norm_sq = lax.psum(jnp.sum(gradient * gradient), ("blk", "rep"))
    update = adam_update(gradient, first_moment, second_moment, weights, norm_sq)
    adam_step = lax.all_gather(update, "rep", axis=2, tiled=True)
    return (hidden, adam_step)


def adam_kernel(
    norm_hbm, hidden_hbm, grad_hbm, near_grad_hbm, first_hbm, second_hbm, weights_hbm, near_first_hbm, near_second_hbm,
    near_weights_hbm, hidden_out, step_out, norm, grad, first_moment, second_moment, weights, update, hidden, norm_sem,
    load_sem, hid_sem, move_sem, store_sem
):
    units, features = grad.shape[2], grad.shape[3]
    tile = units // 4
    sources = (
        (grad_hbm, first_hbm, second_hbm, weights_hbm),
        (near_grad_hbm, near_first_hbm, near_second_hbm, near_weights_hbm),
    )
    held = (grad, first_moment, second_moment, weights)
    steps = [(which, pl.ds(at, tile)) for which in range(2) for at in range(0, units, tile)]
    norm_copy = pltpu.make_async_copy(norm_hbm, norm, norm_sem)
    norm_copy.start()
    loads = []
    for i, (which, rows) in enumerate(steps):
        loads.append([])
        for side in range(2):
            for j in range(4):
                copy = pltpu.make_async_copy(
                    sources[side][j].at[which, rows], held[j].at[side, which, rows], load_sem.at[i, side, j]
                )
                copy.start()
                loads[-1].append(copy)
    band = hidden_hbm.shape[0] // 8
    bands = [pl.ds(i * band, band) for i in range(8)]
    brought = [pltpu.make_async_copy(hidden_hbm.at[rows], hidden.at[rows], hid_sem.at[i]) for i, rows in enumerate(bands)]
    moved = [pltpu.make_async_copy(hidden.at[rows], hidden_out.at[rows], move_sem.at[i]) for i, rows in enumerate(bands)]
    for copy in brought:
        copy.start()
    rep = lax.axis_index("rep")
    columns = [pl.ds(pl.multiple_of(at * features, features), features) for at in (rep, 1 - rep)]
    norm_copy.wait()
    scale = jnp.minimum(1.0, clip_norm / jnp.sqrt(norm[0:1, 0:1]))
    stores = []
    for i, (which, rows) in enumerate(steps):
        for side in range(2):
            for copy in loads[i][4 * side : 4 * side + 4]:
                copy.wait()
            clipped = grad[side, which, rows, :] * scale
            moment = beta_one * first_moment[side, which, rows, :] + (1.0 - beta_one) * clipped
            square = beta_two * second_moment[side, which, rows, :] + (1.0 - beta_two) * clipped * clipped
            moment = moment * (1.0 / (1.0 - beta_one**step_count))
            square = square * (1.0 / (1.0 - beta_two**step_count))
            decay = decay_rate * weights[side, which, rows, :].astype(jnp.float32)
            update[which, rows, columns[side]] = moment / (square * lax.rsqrt(square) + adam_eps) + decay
        stores.append(pltpu.make_async_copy(update.at[which, rows], step_out.at[which, rows], store_sem.at[i]))
        stores[-1].start()
        brought[i].wait()
        moved[i].start()
    for copy in moved + stores:
        copy.wait()


def adam_all(norm_sq, hidden, own, other):
    pair, units, features = own[0].shape
    f32, dma = jnp.float32, pltpu.SemaphoreType.DMA
    anywhere = pl.BlockSpec(memory_space=pl.ANY)
    hbm = pl.BlockSpec(memory_space=pltpu.HBM)
    both = (2, pair, units, features)
    return pl.pallas_call(
        adam_kernel,
        out_shape=(
            jax.ShapeDtypeStruct(hidden.shape, hidden.dtype),
            jax.ShapeDtypeStruct((pair, units, 2 * features), f32),
        ),
        in_specs=[hbm, hbm, hbm, hbm] + [anywhere] * 6,
        out_specs=(hbm, hbm),
        scratch_shapes=[
            pltpu.VMEM((8, 128), f32),
            pltpu.VMEM(both, f32),
            pltpu.VMEM(both, f32),
            pltpu.VMEM(both, f32),
            pltpu.VMEM(both, jnp.bfloat16),
            pltpu.VMEM((pair, units, 2 * features), f32),
            pltpu.VMEM(hidden.shape, hidden.dtype),
            dma, dma((8, 2, 4)), dma((8,)), dma((8,)), dma((8,)),
        ],
        compiler_params=pltpu.CompilerParams(vmem_limit_bytes=63 * 1024 * 1024),
    )(norm_sq, hidden, own[0], other[0], own[1], own[2], own[3], other[1], other[2], other[3])


def cycle_kernel(
    tokens_hbm, grad_hbm, weights_hbm, hidden_hbm, sum_hbm, other_sum, norm_ref,
    tok, tok_near, incoming_ref, hid, mine, other, grads_out, grads_in, x_out, x_in, z_in, sums, own_sum, squares, slots,
    load_sem, hid_sem, ag_recv, inner_send, outer_send, x_send, y_send, y_recv, near_send, near_recv, tok_sem,
    g_send, g_recv, xr_send, xr_recv, zr_send, zr_recv, swap_send, swap_recv, sum_sem, norm_send, norm_recv
):
    devices = lax.axis_size("blk")
    units, features = weights_hbm.shape[1], weights_hbm.shape[2]
    token_count = tok.shape[1]
    part = units // 2
    step = part // 2
    blk, rep, group = lax.axis_index("blk"), lax.axis_index("rep"), lax.axis_index("groups")
    z, x = blk // 2, blk % 2
    end = 1 - ((z + 1) // 2) % 2
    turn = 1 - 2 * (z // 2)
    is_end, is_mid = end == 1, end == 0
    mesh_ids = pl.DeviceIdType.MESH
    near = {"rep": 1 - rep}
    across = {"groups": 1 - group}
    beside = {"blk": 2 * z + 1 - x}
    inner = {"blk": 2 * (z + turn) + x}
    outer = {"blk": 2 * (z - turn * (1 - end)) + x}
    third_z = z + turn * (4 * end - 1)

    def panel(visit, col):
        at = z + turn * visit if visit < 3 else third_z
        return 2 * at + (x if col == 0 else 1 - x)

    row_at = [pl.multiple_of(group * part, part), pl.multiple_of((1 - group) * part, part)]

    def rows_of(half, sub):
        if sub == 2:
            return pl.ds(row_at[half], part)
        return pl.ds(pl.multiple_of(row_at[half] + sub * step, step), step)

    def within(sub):
        return pl.ds(0, part) if sub == 2 else pl.ds(sub * step, step)

    own_at = pl.multiple_of(rep * features, features)
    other_at = pl.multiple_of((1 - rep) * features, features)

    loads = [
        pltpu.make_async_copy(tokens_hbm.at[:, pl.ds(own_at, features)], tok.at[0], load_sem.at[0]),
        pltpu.make_async_copy(tokens_hbm.at[:, pl.ds(other_at, features)], tok.at[1], load_sem.at[1]),
        pltpu.make_async_copy(weights_hbm, mine.at[blk], load_sem.at[2]),
        pltpu.make_async_copy(grad_hbm, incoming_ref, load_sem.at[3]),
    ]
    for copy in loads:
        copy.start()

    members = 2 * devices
    me = blk * 2 + rep

    def member(by):
        peer = (me + by) % members
        return {"blk": peer // 2, "rep": peer % 2}

    barrier = pltpu.get_barrier_semaphore()
    for by in range(1, members):
        pl.semaphore_signal(barrier, inc=1, device_id=member(by), device_id_type=mesh_ids)
    pl.semaphore_signal(barrier, inc=1, device_id=across, device_id_type=mesh_ids)
    pl.semaphore_wait(barrier, members)

    started, line_sends = [], {"E": [], "M": []}
    only = {"E": is_end, "M": is_mid}

    def send(source, target, send_sem, recv_sem, peer, keep=None):
        copy = pltpu.make_async_remote_copy(
            src_ref=source, dst_ref=target, send_sem=send_sem, recv_sem=recv_sem, device_id=peer, device_id_type=mesh_ids
        )
        copy.start()
        if keep is not None:
            keep.append(copy)
        return copy

    def arrive(target, sem, peer):
        pltpu.make_async_remote_copy(
            src_ref=target, dst_ref=target, send_sem=sem, recv_sem=sem, device_id=peer, device_id_type=mesh_ids
        ).wait_recv()

    def departed(ref, sem):
        pltpu.make_async_remote_copy(
            src_ref=ref, dst_ref=ref, send_sem=sem, recv_sem=sem, device_id=inner, device_id_type=mesh_ids
        ).wait_send()

    def piece(q, half, sub):
        return mine.at[q, :, rows_of(half, sub)]

    def own_piece(sub):
        return weights_hbm.at[:, rows_of(0, sub)]

    def line_send(role, outward, visit, col, sub):
        q = panel(visit, col)
        source = own_piece(sub) if visit == 0 and col == 0 else piece(q, 0, sub)
        sems = outer_send if outward else inner_send
        send(source, piece(q, 0, sub), sems.at[q, sub], ag_recv.at[q, sub], outer if outward else inner)
        line_sends[role].append((sems, visit, col, sub))

    def wait_piece(q, sub):
        arrive(piece(q, 0, sub), ag_recv.at[q, sub], inner)

    def from_x(sub):
        wait_piece(panel(0, 1), sub)

    def own_inner(col, sub, role):
        @pl.when(only[role])
        def _():
            line_send(role, False, 0, col, sub)

    def own_outer(col, sub):
        @pl.when(is_mid)
        def _():
            line_send("M", True, 0, col, sub)

    def from_inner(visit, col, sub, role):
        @pl.when(only[role])
        def _():
            wait_piece(panel(visit, col), sub)
            if role == "M":
                line_send("M", True, visit, col, sub)

    def from_outer(col, sub):
        @pl.when(is_mid)
        def _():
            wait_piece(panel(3, col), sub)
            line_send("M", False, 3, col, sub)

    def y_out(visit, col, sub):
        q = panel(visit, col)
        send(piece(q, 0, sub), piece(q, 0, sub), y_send.at[q, sub], y_recv.at[q, sub], across, started)

    def near_out(visit, col, half, sub):
        q = panel(visit, col)
        if half == 1:
            for i in (0, 1) if sub == 2 else (sub,):
                arrive(piece(q, 1, i), y_recv.at[q, i], across)
        rows = rows_of(half, sub)
        send(
            mine.at[q, :, rows], other.at[q, :, rows], near_send.at[q, half, sub % 2], near_recv.at[q, half, sub % 2],
            near, started,
        )

    tile = min(token_count, 256)
    across_features = (((1,), (1,)), ((), ()))
    across_tokens = (((0,), (0,)), ((), ()))
    hid_copies, g_copies, x_copies, ring_at = [], [], [], {}
    ring = grads_out.shape[0]

    def forward(visit, col, half, sub):
        q = panel(visit, col)
        unit_rows, cut = rows_of(half, sub), within(sub)
        arrive(other.at[q, :, unit_rows], near_recv.at[q, half, sub % 2], near)
        slot = (blk - q + devices) % devices
        columns = pl.ds(pl.multiple_of(slot * units + unit_rows.start, 128), unit_rows.size)
        if len(hid_copies) >= 2:
            hid_copies[-2].wait()
        stage = hid.at[len(hid_copies) % 2, :, cut]
        if len(g_copies) >= ring:
            g_copies[-ring].wait_send()
        for i in (0, 1) if sub == 2 else (sub,):
            ring_at[visit, col, half, i] = len(g_copies) % ring
        grads = grads_out.at[len(g_copies) % ring, :, :, cut]

        @pl.loop(0, token_count // tile)
        def _(t):
            rows = pl.ds(pl.multiple_of(t * tile, tile), tile)
            own_tokens, other_tokens = tok[0, rows, :], tok[1, rows, :]

            def product(which):
                return lax.dot_general(
                    own_tokens, mine[q, which, unit_rows, :], across_features, preferred_element_type=jnp.float32
                ) + lax.dot_general(
                    other_tokens, other[q, which, unit_rows, :], across_features, preferred_element_type=jnp.float32
                )

            gate, upper = product(0), product(1)
            incoming = incoming_ref[rows, columns].astype(jnp.float32)
            sigma = jax.nn.sigmoid(gate)
            activated = gate * sigma
            stage[rows, :] = (activated * upper).astype(jnp.bfloat16)
            grads[0, rows, :] = (incoming * upper * sigma * (1.0 + gate * (1.0 - sigma))).astype(jnp.bfloat16)
            grads[1, rows, :] = (incoming * activated).astype(jnp.bfloat16)

        copy = pltpu.make_async_copy(stage, hidden_hbm.at[:, columns], hid_sem.at[len(hid_copies) % 2])
        copy.start()
        hid_copies.append(copy)
        send(
            grads, grads_in.at[visit, col, half, :, :, cut], g_send.at[visit, col, half, sub % 2],
            g_recv.at[visit, col, half, sub % 2], near, g_copies,
        )

    def got_grads(visit, col, half, sub):
        arrive(grads_in.at[visit, col, half, :, :, within(sub)], g_recv.at[visit, col, half, sub % 2], near)

    def gradient_term(visit, col, half, sub, which):
        grads = grads_out.at[ring_at[visit, col, half, sub % 2]]
        got = grads_in.at[visit, col, half]
        rows = within(sub)
        return lax.dot_general(
            grads[which, :, rows], tok[0], across_tokens, preferred_element_type=jnp.float32
        ) + lax.dot_general(got[which, :, rows], tok_near[...], across_tokens, preferred_element_type=jnp.float32)

    def give(visit, half, sub):
        got_grads(visit, 1, half, sub)
        for i in (0, 1) if sub == 2 else (sub,):
            for which in range(2):
                target = x_out.at[visit, half, which, within(i)]
                target[...] = gradient_term(visit, 1, half, i, which).astype(jnp.bfloat16)
                send(
                    target, x_in.at[visit, half, which, within(i)], xr_send.at[visit, half, i, which],
                    xr_recv.at[visit, half, i, which], beside, x_copies,
                )

    def total_at(visit, half, which, sub):
        if visit == 0:
            return own_sum.at[which, rows_of(half, sub)]
        return sums.at[visit - 1, half, which, within(sub)]

    def term(visit, half, sub):
        got_grads(visit, 0, half, sub)
        for which in range(2):
            total_at(visit, half, which, sub)[...] = gradient_term(visit, 0, half, sub, which)

    def from_beside(visit, half, sub, which):
        arrive(x_in.at[visit, half, which, within(sub)], xr_recv.at[visit, half, sub, which], beside)
        return x_in[visit, half, which, within(sub), :].astype(jnp.float32)

    def from_line(slot, half, sub, which):
        arrive(z_in.at[slot, half, which, within(sub)], zr_recv.at[slot, half, sub, which], inner)
        return z_in[slot, half, which, within(sub), :].astype(jnp.float32)

    def add_beside(visit, half, sub):
        def run():
            for which in range(2):
                total_at(visit, half, which, sub)[...] += from_beside(visit, half, sub, which)

        if visit == 0:
            run()
        else:
            pl.when(is_mid)(run)

    def add_outer(half, sub):
        @pl.when(is_mid)
        def _():
            for which in range(2):
                total_at(0, half, which, sub)[...] += from_line(0, half, sub, which)

    def pass_on(visit, half, sub, role):
        @pl.when(only[role])
        def _():
            to = visit - 1 if role == "E" else 3 + visit % 2
            peer = outer if visit == 3 and role == "M" else inner
            for which in range(2):
                if role == "E":
                    added = from_beside(visit, half, sub, which)
                else:
                    added = from_line(visit, half, sub, which)
                target = x_in.at[visit, half, which, within(sub)]
                target[...] = (total_at(visit, half, which, sub)[...] + added).astype(jnp.bfloat16)
                send(
                    target, z_in.at[to, half, which, within(sub)], zr_send.at[visit - 1, half, sub, which],
                    zr_recv.at[to, half, sub, which], peer,
                )

    kept = []

    def finish(half, sub):
        for which in range(2):
            target = total_at(0, half, which, sub)
            total = target[...] + from_line(4, half, sub, which)
            target[...] = total
            folded = jnp.sum((total * total).reshape(step // 8, 8, features), axis=0)
            for lane in range(0, features, 128):
                squares[...] += folded[:, lane : lane + 128]
            rows = rows_of(half, sub)
            send(
                target, other_sum.at[which, rows], swap_send.at[half, sub, which], swap_recv.at[half, sub, which], near,
                started,
            )
            copy = pltpu.make_async_copy(target, sum_hbm.at[which, rows], sum_sem.at[half, sub, which])
            copy.start()
            kept.append(copy)

    def own_start(sub):
        send(own_piece(sub), piece(blk, 0, sub), x_send.at[sub], ag_recv.at[blk, sub], beside, started)

    own_start(0)
    for role in "EM":
        own_inner(0, 0, role)
    own_outer(0, 0)
    own_start(1)
    for half in range(2):
        rows = rows_of(half, 2)
        send(
            weights_hbm.at[:, rows], other.at[blk, :, rows], near_send.at[blk, half, 0], near_recv.at[blk, half, 0], near,
            started,
        )
    loads[1].wait()
    send(tok.at[1], tok_near, tok_sem.at[0], tok_sem.at[1], near, started)
    squares[...] = jnp.zeros_like(squares)
    for copy in (loads[0], loads[2], loads[3]):
        copy.wait()
    arrive(tok_near, tok_sem.at[1], near)

    forward(0, 0, 1, 2)
    own_outer(0, 1)
    own_inner(0, 1, "M")
    own_inner(0, 1, "E")
    from_inner(1, 0, 0, "E")
    forward(0, 0, 0, 2)
    from_x(0)
    near_out(0, 1, 0, 0)
    from_inner(1, 0, 0, "M")
    y_out(1, 0, 0)
    own_inner(1, 0, "M")
    forward(0, 1, 0, 0)
    term(0, 1, 2)
    from_x(1)
    own_inner(1, 1, "E")
    own_inner(1, 1, "M")
    from_inner(1, 0, 1, "E")
    own_outer(1, 0)
    near_out(0, 1, 0, 1)
    y_out(0, 1, 1)
    own_inner(1, 0, "E")
    give(0, 0, 0)
    forward(0, 1, 0, 1)
    give(0, 0, 1)
    from_inner(1, 1, 0, "E")
    own_outer(1, 1)
    from_inner(1, 1, 0, "M")
    near_out(1, 1, 0, 0)
    y_out(1, 1, 0)
    forward(1, 1, 0, 0)
    term(0, 0, 2)
    from_outer(1, 1)
    from_inner(1, 1, 1, "M")
    from_inner(1, 0, 1, "M")
    give(1, 0, 0)
    from_inner(1, 1, 1, "E")
    near_out(1, 1, 0, 1)
    y_out(1, 0, 1)
    near_out(1, 1, 1, 0)
    y_out(1, 1, 1)
    from_outer(1, 0)
    near_out(1, 0, 0, 2)
    forward(1, 1, 0, 1)
    forward(1, 0, 0, 2)
    give(1, 0, 1)
    from_inner(2, 1, 1, "M")
    from_outer(0, 0)
    near_out(1, 0, 1, 2)
    forward(1, 0, 1, 2)
    from_outer(0, 1)
    from_inner(2, 1, 0, "M")
    from_inner(2, 1, 0, "E")
    y_out(2, 1, 0)
    from_inner(2, 1, 1, "E")
    term(1, 0, 2)
    pass_on(1, 0, 0, "E")
    forward(1, 1, 1, 0)
    near_out(1, 1, 1, 1)
    near_out(2, 1, 0, 1)
    y_out(2, 1, 1)
    give(1, 1, 0)
    forward(2, 1, 0, 1)
    pass_on(1, 0, 1, "E")
    from_inner(2, 0, 0, "E")
    add_beside(1, 0, 1)
    term(1, 1, 2)
    give(2, 0, 1)
    near_out(2, 1, 0, 0)
    from_inner(3, 1, 1, "E")
    near_out(3, 1, 0, 1)
    from_inner(2, 0, 0, "M")
    from_inner(2, 0, 1, "M")
    from_inner(2, 0, 1, "E")
    add_beside(1, 0, 0)
    y_out(3, 1, 1)
    pass_on(1, 1, 0, "E")
    near_out(2, 0, 0, 2)
    forward(2, 1, 0, 0)
    near_out(2, 1, 1, 2)
    forward(3, 1, 0, 1)
    forward(2, 0, 0, 2)
    from_inner(3, 1, 0, "E")
    y_out(3, 1, 0)
    near_out(3, 1, 0, 0)
    give(2, 0, 0)
    forward(1, 1, 1, 1)
    term(2, 0, 2)
    pass_on(2, 0, 1, "E")
    give(3, 0, 1)
    from_inner(3, 0, 0, "E")
    y_out(3, 0, 0)
    pass_on(2, 0, 0, "E")
    forward(3, 1, 0, 0)
    from_inner(3, 0, 1, "E")
    near_out(3, 0, 0, 2)
    give(3, 0, 0)
    y_out(3, 0, 1)
    near_out(3, 1, 1, 2)
    y_out(2, 0, 0)
    add_outer(0, 0)
    forward(3, 0, 0, 2)
    forward(3, 1, 1, 2)
    term(3, 0, 2)
    add_outer(1, 0)
    pass_on(3, 0, 1, "E")
    add_beside(2, 0, 0)
    pass_on(1, 0, 1, "M")
    give(3, 1, 2)
    near_out(3, 0, 1, 2)
    add_outer(0, 1)
    add_beside(3, 0, 1)
    forward(2, 1, 1, 2)
    pass_on(1, 0, 0, "M")
    add_beside(2, 0, 1)
    pass_on(3, 0, 0, "E")
    y_out(2, 0, 1)
    forward(3, 0, 1, 2)
    give(2, 1, 2)
    term(3, 1, 2)
    y_out(0, 1, 0)
    pass_on(3, 1, 0, "E")
    pass_on(2, 0, 1, "M")
    near_out(2, 0, 1, 2)
    add_beside(3, 0, 0)
    add_beside(0, 0, 0)
    give(1, 1, 1)
    forward(2, 0, 1, 2)
    pass_on(2, 0, 0, "M")
    pass_on(3, 1, 1, "E")
    pass_on(3, 0, 1, "M")
    add_beside(3, 1, 1)
    near_out(0, 1, 1, 2)
    add_beside(0, 0, 1)
    term(2, 1, 2)
    add_beside(2, 1, 0)
    pass_on(2, 1, 0, "E")
    pass_on(2, 1, 0, "M")
    add_beside(2, 1, 1)
    pass_on(3, 0, 0, "M")
    finish(0, 1)
    add_beside(3, 1, 0)
    forward(0, 1, 1, 2)
    pass_on(2, 1, 1, "M")
    pass_on(3, 1, 0, "M")
    give(0, 1, 2)
    add_beside(1, 1, 0)
    pass_on(1, 1, 0, "M")
    finish(0, 0)
    add_beside(1, 1, 1)
    pass_on(2, 1, 1, "E")
    pass_on(3, 1, 1, "M")
    pass_on(1, 1, 1, "M")
    pass_on(1, 1, 1, "E")
    add_beside(0, 1, 0)
    finish(1, 0)
    add_beside(0, 1, 1)
    add_outer(1, 1)
    finish(1, 1)

    slots[me] = squares[...]
    copies = []
    for by in range(1, members):
        send(squares, slots.at[me], norm_send.at[by], norm_recv.at[by], member(by), copies)
    for copy in started + g_copies[-ring:] + x_copies:
        copy.wait_send()
    for visit in range(1, 4):
        for half in range(2):
            for sub in range(2):
                for which in range(2):
                    departed(x_in.at[visit, half, which, within(sub)], zr_send.at[visit - 1, half, sub, which])
    for role in "EM":

        @pl.when(only[role])
        def _():
            for sems, visit, col, sub in line_sends[role]:
                q = panel(visit, col)
                departed(piece(q, 0, sub), sems.at[q, sub])

    for copy in hid_copies[-2:] + kept:
        copy.wait()
    for half in range(2):
        for sub in range(2):
            for which in range(2):
                arrive(other_sum.at[which, rows_of(half, sub)], swap_recv.at[half, sub, which], near)
    for copy in copies:
        copy.wait()
    total = slots[0]
    for i in range(1, members):
        total = total + slots[i]
    norm_ref[...] = jnp.full(norm_ref.shape, jnp.sum(total), jnp.float32)


def cycle_all(tokens, hidden_grad, weights):
    devices = lax.axis_size("blk")
    units, features = weights.shape[1], weights.shape[2]
    token_count = tokens.shape[0]
    part = units // 2
    bf16, f32 = jnp.bfloat16, jnp.float32
    vmem, anywhere = pl.BlockSpec(memory_space=pltpu.VMEM), pl.BlockSpec(memory_space=pl.ANY)
    dma = pltpu.SemaphoreType.DMA
    grads = (2, token_count, part)
    sums = (2, part, features)
    pairs = dma((devices, 2))
    quads = (2, 2, 2)
    return pl.pallas_call(
        cycle_kernel,
        out_shape=(
            jax.ShapeDtypeStruct(hidden_grad.shape, bf16),
            jax.ShapeDtypeStruct((2, units, features), f32),
            jax.ShapeDtypeStruct((2, units, features), f32),
            jax.ShapeDtypeStruct((8, 128), f32),
        ),
        in_specs=[anywhere] * 3,
        out_specs=(anywhere, anywhere, anywhere, vmem),
        scratch_shapes=[
            pltpu.VMEM((2, token_count, features), bf16),
            pltpu.VMEM((token_count, features), bf16),
            pltpu.VMEM(hidden_grad.shape, bf16),
            pltpu.VMEM((2, token_count, part), bf16),
            pltpu.VMEM((devices, 2, units, features), bf16),
            pltpu.VMEM((devices, 2, units, features), bf16),
            pltpu.VMEM((RING,) + grads, bf16),
            pltpu.VMEM((4, 2, 2) + grads, bf16),
            pltpu.VMEM((4, 2) + sums, bf16),
            pltpu.VMEM((4, 2) + sums, bf16),
            pltpu.VMEM((5, 2) + sums, bf16),
            pltpu.VMEM((3, 2) + sums, f32),
            pltpu.VMEM((2, units, features), f32),
            pltpu.VMEM((8, 128), f32),
            pltpu.VMEM((2 * devices, 8, 128), f32),
            dma((4,)), dma((2,)), pairs, pairs, pairs, dma((2,)), pairs, pairs,
            dma((devices, 2, 2)), dma((devices, 2, 2)), dma((2,)),
            dma((4,) + quads), dma((4,) + quads), dma((4,) + quads), dma((4,) + quads), dma((3,) + quads),
            dma((5,) + quads), dma(quads), dma(quads), dma(quads), dma((2 * devices,)), dma((2 * devices,)),
        ],
        compiler_params=pltpu.CompilerParams(
            collective_id=1, has_side_effects=True, vmem_limit_bytes=58 * 1024 * 1024
        ),
    )(tokens, hidden_grad, weights)


def on_ring(tokens, hidden_grad, weights, first_moment, second_moment):
    def partner(value):
        return lax.ppermute(value, "rep", [(0, 1), (1, 0)])

    hidden, gradient, other_gradient, norm_sq = cycle_all(tokens, hidden_grad, weights)
    own = (first_moment, second_moment, weights)
    other = tuple(partner(value) for value in own)
    return adam_all(norm_sq, hidden, (gradient,) + own, (other_gradient,) + other)


def solution(mesh):
    placed = (
        P(("groups", "blk", "rep"), None),
        P(("groups", "blk", "rep"), None),
        P(None, "blk", "rep"),
        P(None, ("groups", "blk"), "rep"),
        P(None, ("groups", "blk"), "rep"),
    )
    devices = mesh.shape["blk"]

    def program(tokens, hidden_grad, weights, first_moment, second_moment):
        slots = hidden_grad.shape[1] * devices // weights.shape[1]
        whole_cycle = slots == devices and devices == 8 and mesh.shape["rep"] == 2 and mesh.shape["groups"] == 2
        step = jax.shard_map(
            on_ring if whole_cycle else on_device,
            mesh=mesh,
            in_specs=placed,
            out_specs=(P(("groups", "blk", "rep"), None), P(None, ("groups", "blk"), None)),
            check_vma=False,
        )
        return step(tokens, hidden_grad, weights, first_moment, second_moment)

    return program
```

```python
import jax
import jax.numpy as jnp
from jax import lax
from jax.experimental import pallas as pl
from jax.experimental.pallas import tpu as pltpu
from jax.sharding import PartitionSpec as P

clip_norm = 1.0
beta_one = 0.9
beta_two = 0.95
step_count = 10.0
adam_eps = 1e-08
decay_rate = 0.1
RING = 6


def shifted(value, axis, by):
    devices = lax.axis_size(axis)
    return lax.ppermute(value, axis, [(i, (i + by) % devices) for i in range(devices)])


def swiglu_terms(tokens, incoming_grad, gate_rows, up_rows):
    contract = (((1,), (1,)), ((), ()))
    gate = lax.dot_general(tokens, gate_rows, contract, preferred_element_type=jnp.float32)
    upper = lax.dot_general(tokens, up_rows, contract, preferred_element_type=jnp.float32)
    sigma = jax.nn.sigmoid(gate)
    activated = gate * sigma
    hidden = (activated * upper).astype(jnp.bfloat16)
    incoming = incoming_grad.astype(jnp.float32)
    gate_grad = (incoming * upper * sigma * (1.0 + gate * (1.0 - sigma))).astype(jnp.bfloat16)
    up_grad = (incoming * activated).astype(jnp.bfloat16)
    return (hidden, gate_grad, up_grad)


def adam_update(gradient, first_moment, second_moment, weights, norm_sq):
    clip_scale = jnp.minimum(1.0, clip_norm / jnp.sqrt(norm_sq))
    clipped = gradient * clip_scale
    first = beta_one * first_moment + (1.0 - beta_one) * clipped
    second = beta_two * second_moment + (1.0 - beta_two) * clipped * clipped
    first_hat = first / (1.0 - beta_one**step_count)
    second_hat = second / (1.0 - beta_two**step_count)
    return first_hat / (jnp.sqrt(second_hat) + adam_eps) + decay_rate * weights.astype(jnp.float32)


def on_device(tokens, hidden_grad, weights, first_moment, second_moment):
    unit_count = weights.shape[1]
    token_count = tokens.shape[0]
    slot_count = hidden_grad.shape[1] // unit_count
    own_full = lax.all_gather(weights, "rep", axis=2, tiled=True)
    slot_grads = jnp.swapaxes(hidden_grad.reshape(token_count, slot_count, unit_count), 0, 1)
    contract = (((1,), (0,)), ((), ()))

    def grad_term(gate_grad, up_grad):
        paired = jnp.stack([gate_grad, up_grad], axis=0)
        return lax.dot_general(paired, tokens, contract, preferred_element_type=jnp.float32)

    zero_sums = jnp.zeros((2, unit_count, tokens.shape[1]), jnp.float32)

    def visit(panel_rows, slot_grad):
        hidden, gate_grad, up_grad = swiglu_terms(tokens, slot_grad, panel_rows[0], panel_rows[1])
        arrived = shifted(panel_rows, "blk", 1)
        return (arrived, (hidden, gate_grad, up_grad))

    _, (hidden_slots, gate_slots, up_slots) = lax.scan(visit, own_full, slot_grads)

    def collect(running, grads_pair):
        arrived = shifted(running, "blk", -1)
        return (arrived + grad_term(grads_pair[0], grads_pair[1]), None)

    owned_sums, _ = lax.scan(collect, zero_sums, (gate_slots, up_slots), reverse=True)
    hidden = jnp.swapaxes(hidden_slots, 0, 1).reshape(token_count, slot_count * unit_count)
    gradient = lax.psum_scatter(owned_sums, "rep", scatter_dimension=2, tiled=True)
    norm_sq = lax.psum(jnp.sum(gradient * gradient), ("blk", "rep"))
    update = adam_update(gradient, first_moment, second_moment, weights, norm_sq)
    adam_step = lax.all_gather(update, "rep", axis=2, tiled=True)
    return (hidden, adam_step)


def adam_kernel(
    norm_hbm, hidden_hbm, grad_hbm, near_grad_hbm, first_hbm, second_hbm, weights_hbm, near_first_hbm, near_second_hbm,
    near_weights_hbm, hidden_out, step_out, norm, grad, first_moment, second_moment, weights, update, hidden, norm_sem,
    load_sem, hid_sem, move_sem, store_sem
):
    units, features = grad.shape[2], grad.shape[3]
    tile = units // 4
    sources = (
        (grad_hbm, first_hbm, second_hbm, weights_hbm),
        (near_grad_hbm, near_first_hbm, near_second_hbm, near_weights_hbm),
    )
    held = (grad, first_moment, second_moment, weights)
    steps = [(which, pl.ds(at, tile)) for which in range(2) for at in range(0, units, tile)]
    norm_copy = pltpu.make_async_copy(norm_hbm, norm, norm_sem)
    norm_copy.start()
    loads = []
    for i, (which, rows) in enumerate(steps):
        loads.append([])
        for side in range(2):
            for j in range(4):
                copy = pltpu.make_async_copy(
                    sources[side][j].at[which, rows], held[j].at[side, which, rows], load_sem.at[i, side, j]
                )
                copy.start()
                loads[-1].append(copy)
    band = hidden_hbm.shape[0] // 8
    bands = [pl.ds(i * band, band) for i in range(8)]
    brought = [pltpu.make_async_copy(hidden_hbm.at[rows], hidden.at[rows], hid_sem.at[i]) for i, rows in enumerate(bands)]
    moved = [pltpu.make_async_copy(hidden.at[rows], hidden_out.at[rows], move_sem.at[i]) for i, rows in enumerate(bands)]
    for copy in brought:
        copy.start()
    rep = lax.axis_index("rep")
    columns = [pl.ds(pl.multiple_of(at * features, features), features) for at in (rep, 1 - rep)]
    norm_copy.wait()
    scale = jnp.minimum(1.0, clip_norm / jnp.sqrt(norm[0:1, 0:1]))
    stores = []
    for i, (which, rows) in enumerate(steps):
        for side in range(2):
            for copy in loads[i][4 * side : 4 * side + 4]:
                copy.wait()
            clipped = grad[side, which, rows, :] * scale
            moment = beta_one * first_moment[side, which, rows, :] + (1.0 - beta_one) * clipped
            square = beta_two * second_moment[side, which, rows, :] + (1.0 - beta_two) * clipped * clipped
            moment = moment * (1.0 / (1.0 - beta_one**step_count))
            square = square * (1.0 / (1.0 - beta_two**step_count))
            decay = decay_rate * weights[side, which, rows, :].astype(jnp.float32)
            update[which, rows, columns[side]] = moment / (square * lax.rsqrt(square) + adam_eps) + decay
        stores.append(pltpu.make_async_copy(update.at[which, rows], step_out.at[which, rows], store_sem.at[i]))
        stores[-1].start()
        brought[i].wait()
        moved[i].start()
    for copy in moved + stores:
        copy.wait()


def adam_all(norm_sq, hidden, own, other):
    pair, units, features = own[0].shape
    f32, dma = jnp.float32, pltpu.SemaphoreType.DMA
    anywhere = pl.BlockSpec(memory_space=pl.ANY)
    hbm = pl.BlockSpec(memory_space=pltpu.HBM)
    both = (2, pair, units, features)
    return pl.pallas_call(
        adam_kernel,
        out_shape=(
            jax.ShapeDtypeStruct(hidden.shape, hidden.dtype),
            jax.ShapeDtypeStruct((pair, units, 2 * features), f32),
        ),
        in_specs=[hbm, hbm, hbm, hbm] + [anywhere] * 6,
        out_specs=(hbm, hbm),
        scratch_shapes=[
            pltpu.VMEM((8, 128), f32),
            pltpu.VMEM(both, f32),
            pltpu.VMEM(both, f32),
            pltpu.VMEM(both, f32),
            pltpu.VMEM(both, jnp.bfloat16),
            pltpu.VMEM((pair, units, 2 * features), f32),
            pltpu.VMEM(hidden.shape, hidden.dtype),
            dma, dma((8, 2, 4)), dma((8,)), dma((8,)), dma((8,)),
        ],
        compiler_params=pltpu.CompilerParams(vmem_limit_bytes=63 * 1024 * 1024),
    )(norm_sq, hidden, own[0], other[0], own[1], own[2], own[3], other[1], other[2], other[3])


def cycle_kernel(
    tokens_hbm, grad_hbm, weights_hbm, hidden_hbm, sum_hbm, other_sum, norm_ref,
    tok, tok_near, incoming_ref, hid, mine, other, grads_out, grads_in, x_out, x_in, z_in, sums, own_sum, squares, slots,
    load_sem, hid_sem, ag_recv, inner_send, outer_send, x_send, y_send, y_recv, near_send, near_recv, tok_sem,
    g_send, g_recv, xr_send, xr_recv, zr_send, zr_recv, swap_send, swap_recv, sum_sem, norm_send, norm_recv
):
    devices = lax.axis_size("blk")
    units, features = weights_hbm.shape[1], weights_hbm.shape[2]
    token_count = tok.shape[1]
    part = units // 2
    step = part // 2
    blk, rep, group = lax.axis_index("blk"), lax.axis_index("rep"), lax.axis_index("groups")
    z, x = blk // 2, blk % 2
    end = 1 - ((z + 1) // 2) % 2
    turn = 1 - 2 * (z // 2)
    is_end, is_mid = end == 1, end == 0
    mesh_ids = pl.DeviceIdType.MESH
    near = {"rep": 1 - rep}
    across = {"groups": 1 - group}
    beside = {"blk": 2 * z + 1 - x}
    inner = {"blk": 2 * (z + turn) + x}
    outer = {"blk": 2 * (z - turn * (1 - end)) + x}
    third_z = z + turn * (4 * end - 1)

    def panel(visit, col):
        at = z + turn * visit if visit < 3 else third_z
        return 2 * at + (x if col == 0 else 1 - x)

    row_at = [pl.multiple_of(group * part, part), pl.multiple_of((1 - group) * part, part)]

    def rows_of(half, sub):
        if sub == 2:
            return pl.ds(row_at[half], part)
        return pl.ds(pl.multiple_of(row_at[half] + sub * step, step), step)

    def within(sub):
        return pl.ds(0, part) if sub == 2 else pl.ds(sub * step, step)

    own_at = pl.multiple_of(rep * features, features)
    other_at = pl.multiple_of((1 - rep) * features, features)

    loads = [
        pltpu.make_async_copy(tokens_hbm.at[:, pl.ds(own_at, features)], tok.at[0], load_sem.at[0]),
        pltpu.make_async_copy(tokens_hbm.at[:, pl.ds(other_at, features)], tok.at[1], load_sem.at[1]),
        pltpu.make_async_copy(weights_hbm, mine.at[blk], load_sem.at[2]),
        pltpu.make_async_copy(grad_hbm, incoming_ref, load_sem.at[3]),
    ]
    for copy in loads:
        copy.start()

    members = 2 * devices
    me = blk * 2 + rep

    def member(by):
        peer = (me + by) % members
        return {"blk": peer // 2, "rep": peer % 2}

    barrier = pltpu.get_barrier_semaphore()
    for by in range(1, members):
        pl.semaphore_signal(barrier, inc=1, device_id=member(by), device_id_type=mesh_ids)
    pl.semaphore_signal(barrier, inc=1, device_id=across, device_id_type=mesh_ids)
    pl.semaphore_wait(barrier, members)

    started, inside = [], []

    def send(source, target, send_sem, recv_sem, peer, keep=None):
        copy = pltpu.make_async_remote_copy(
            src_ref=source, dst_ref=target, send_sem=send_sem, recv_sem=recv_sem, device_id=peer, device_id_type=mesh_ids
        )
        copy.start()
        if keep is not None:
            keep.append(copy)
        return copy

    def arrive(target, sem, peer):
        pltpu.make_async_remote_copy(
            src_ref=target, dst_ref=target, send_sem=sem, recv_sem=sem, device_id=peer, device_id_type=mesh_ids
        ).wait_recv()

    def departed(ref, sem):
        pltpu.make_async_remote_copy(
            src_ref=ref, dst_ref=ref, send_sem=sem, recv_sem=sem, device_id=inner, device_id_type=mesh_ids
        ).wait_send()

    def piece(q, half, sub):
        return mine.at[q, :, rows_of(half, sub)]

    def own_piece(sub):
        return weights_hbm.at[:, rows_of(0, sub)]

    def line_send(outward, visit, col, sub, keep=inside):
        q = panel(visit, col)
        source = own_piece(sub) if visit == 0 and col == 0 else piece(q, 0, sub)
        sems = outer_send if outward else inner_send
        send(source, piece(q, 0, sub), sems.at[q, sub], ag_recv.at[q, sub], outer if outward else inner, keep)

    def wait_piece(q, sub):
        arrive(piece(q, 0, sub), ag_recv.at[q, sub], inner)

    def from_x(sub):
        wait_piece(panel(0, 1), sub)

    def own_inner(col, sub):
        line_send(False, 0, col, sub)

    def own_outer(col, sub):
        line_send(True, 0, col, sub)

    def arrives(visit, col, sub):
        wait_piece(panel(visit, col), sub)

    def relay_out(visit, col, sub):
        wait_piece(panel(visit, col), sub)
        line_send(True, visit, col, sub)

    def relay_in(col, sub):
        wait_piece(panel(3, col), sub)
        line_send(False, 3, col, sub)

    def y_out(visit, col, sub):
        q = panel(visit, col)
        send(piece(q, 0, sub), piece(q, 0, sub), y_send.at[q, sub], y_recv.at[q, sub], across, inside)

    def near_out(visit, col, half, sub):
        q = panel(visit, col)
        if half == 1:
            for i in (0, 1) if sub == 2 else (sub,):
                arrive(piece(q, 1, i), y_recv.at[q, i], across)
        rows = rows_of(half, sub)
        send(
            mine.at[q, :, rows], other.at[q, :, rows], near_send.at[q, half, sub % 2], near_recv.at[q, half, sub % 2],
            near, inside,
        )

    tile = min(token_count, 128)
    across_features = (((1,), (1,)), ((), ()))
    across_tokens = (((0,), (0,)), ((), ()))
    hid_copies, g_copies, kept, ring_at = [], [], [], {}
    ring = grads_out.shape[0]

    def forward(visit, col, half, sub):
        q = panel(visit, col)
        unit_rows, cut = rows_of(half, sub), within(sub)
        arrive(other.at[q, :, unit_rows], near_recv.at[q, half, sub % 2], near)
        slot = (blk - q + devices) % devices
        columns = pl.ds(pl.multiple_of(slot * units + unit_rows.start, 128), unit_rows.size)
        if len(hid_copies) >= 2:
            hid_copies[-2].wait()
        stage = hid.at[len(hid_copies) % 2, :, cut]
        if len(g_copies) >= ring:
            g_copies[-ring].wait_send()
        for i in (0, 1) if sub == 2 else (sub,):
            ring_at[visit, col, half, i] = len(g_copies) % ring
        grads = grads_out.at[len(g_copies) % ring, :, :, cut]

        @pl.loop(0, token_count // tile)
        def _(t):
            rows = pl.ds(pl.multiple_of(t * tile, tile), tile)
            own_tokens, other_tokens = tok[0, rows, :], tok[1, rows, :]

            def product(which):
                return lax.dot_general(
                    own_tokens, mine[q, which, unit_rows, :], across_features, preferred_element_type=jnp.float32
                ) + lax.dot_general(
                    other_tokens, other[q, which, unit_rows, :], across_features, preferred_element_type=jnp.float32
                )

            gate, upper = product(0), product(1)
            incoming = incoming_ref[rows, columns].astype(jnp.float32)
            sigma = jax.nn.sigmoid(gate)
            activated = gate * sigma
            stage[rows, :] = (activated * upper).astype(jnp.bfloat16)
            grads[0, rows, :] = (incoming * upper * sigma * (1.0 + gate * (1.0 - sigma))).astype(jnp.bfloat16)
            grads[1, rows, :] = (incoming * activated).astype(jnp.bfloat16)

        copy = pltpu.make_async_copy(stage, hidden_hbm.at[:, columns], hid_sem.at[len(hid_copies) % 2])
        copy.start()
        hid_copies.append(copy)
        send(
            grads, grads_in.at[visit, col, half, :, :, cut], g_send.at[visit, col, half, sub % 2],
            g_recv.at[visit, col, half, sub % 2], near, g_copies,
        )

    def got_grads(visit, col, half, sub):
        arrive(grads_in.at[visit, col, half, :, :, within(sub)], g_recv.at[visit, col, half, sub % 2], near)

    def gradient_term(visit, col, half, sub, which):
        grads = grads_out.at[ring_at[visit, col, half, sub % 2]]
        got = grads_in.at[visit, col, half]
        rows = within(sub)
        return lax.dot_general(
            grads[which, :, rows], tok[0], across_tokens, preferred_element_type=jnp.float32
        ) + lax.dot_general(got[which, :, rows], tok_near[...], across_tokens, preferred_element_type=jnp.float32)

    def give(visit, half, sub):
        got_grads(visit, 1, half, sub)
        for i in (0, 1) if sub == 2 else (sub,):
            for which in range(2):
                target = x_out.at[visit, half, which, within(i)]
                target[...] = gradient_term(visit, 1, half, i, which).astype(jnp.bfloat16)
                send(
                    target, x_in.at[visit, half, which, within(i)], xr_send.at[visit, half, i, which],
                    xr_recv.at[visit, half, i, which], beside, inside,
                )

    def total_at(visit, half, which, sub):
        if visit == 0:
            return own_sum.at[which, rows_of(half, sub)]
        return sums.at[visit - 1, half, which, within(sub)]

    def term(visit, half, sub):
        got_grads(visit, 0, half, sub)
        for which in range(2):
            total_at(visit, half, which, sub)[...] = gradient_term(visit, 0, half, sub, which)

    def from_beside(visit, half, sub, which):
        arrive(x_in.at[visit, half, which, within(sub)], xr_recv.at[visit, half, sub, which], beside)
        return x_in[visit, half, which, within(sub), :].astype(jnp.float32)

    def from_line(slot, half, sub, which):
        arrive(z_in.at[slot, half, which, within(sub)], zr_recv.at[slot, half, sub, which], inner)
        return z_in[slot, half, which, within(sub), :].astype(jnp.float32)

    def add_beside(visit, half, sub):
        for which in range(2):
            total_at(visit, half, which, sub)[...] += from_beside(visit, half, sub, which)

    def add_outer(half, sub):
        for which in range(2):
            total_at(0, half, which, sub)[...] += from_line(0, half, sub, which)

    def pass_on(visit, half, sub, at_end):
        to = visit - 1 if at_end else 3 + visit % 2
        peer = outer if visit == 3 and not at_end else inner
        for which in range(2):
            if at_end:
                added = from_beside(visit, half, sub, which)
            else:
                added = from_line(visit, half, sub, which)
            target = x_in.at[visit, half, which, within(sub)]
            target[...] = (total_at(visit, half, which, sub)[...] + added).astype(jnp.bfloat16)
            send(
                target, z_in.at[to, half, which, within(sub)], zr_send.at[visit - 1, half, sub, which],
                zr_recv.at[to, half, sub, which], peer, inside,
            )

    def finish(half, sub):
        for which in range(2):
            target = total_at(0, half, which, sub)
            total = target[...] + from_line(4, half, sub, which)
            target[...] = total
            folded = jnp.sum((total * total).reshape(step // 8, 8, features), axis=0)
            for lane in range(0, features, 128):
                squares[...] += folded[:, lane : lane + 128]
            rows = rows_of(half, sub)
            send(
                target, other_sum.at[which, rows], swap_send.at[half, sub, which], swap_recv.at[half, sub, which], near,
                inside,
            )
            copy = pltpu.make_async_copy(target, sum_hbm.at[which, rows], sum_sem.at[half, sub, which])
            copy.start()
            kept.append(copy)

    def own_start(sub):
        send(own_piece(sub), piece(blk, 0, sub), x_send.at[sub], ag_recv.at[blk, sub], beside, started)

    own_start(0)
    line_send(False, 0, 0, 0, started)

    @pl.when(is_mid)
    def _():
        line_send(True, 0, 0, 0, None)

    own_start(1)
    for half in range(2):
        rows = rows_of(half, 2)
        send(
            weights_hbm.at[:, rows], other.at[blk, :, rows], near_send.at[blk, half, 0], near_recv.at[blk, half, 0], near,
            started,
        )
    loads[1].wait()
    send(tok.at[1], tok_near, tok_sem.at[0], tok_sem.at[1], near, started)
    squares[...] = jnp.zeros_like(squares)
    for copy in (loads[0], loads[2], loads[3]):
        copy.wait()
    arrive(tok_near, tok_sem.at[1], near)

    def close():
        slots[me] = squares[...]
        copies = []
        for by in range(1, members):
            send(squares, slots.at[me], norm_send.at[by], norm_recv.at[by], member(by), copies)
        for copy in inside + g_copies[-ring:]:
            copy.wait_send()
        for copy in hid_copies[-2:] + kept:
            copy.wait()
        for half in range(2):
            for sub in range(2):
                for which in range(2):
                    arrive(other_sum.at[which, rows_of(half, sub)], swap_recv.at[half, sub, which], near)
        for copy in copies:
            copy.wait()
        total = slots[0]
        for i in range(1, members):
            total = total + slots[i]
        norm_ref[...] = jnp.full(norm_ref.shape, jnp.sum(total), jnp.float32)

    @pl.when(is_end)
    def _():
        own_inner(0, 1)
        forward(0, 0, 0, 2)
        forward(0, 0, 1, 2)
        arrives(1, 0, 0)
        y_out(1, 0, 0)
        from_x(0)
        near_out(0, 1, 0, 0)
        forward(0, 1, 0, 0)
        from_x(1)
        own_inner(1, 1)
        arrives(1, 0, 1)
        y_out(1, 0, 1)
        near_out(0, 1, 0, 1)
        own_inner(1, 0)
        near_out(1, 0, 0, 2)
        give(0, 0, 0)
        forward(0, 1, 0, 1)
        forward(1, 0, 0, 2)
        arrives(1, 1, 0)
        y_out(0, 1, 1)
        term(1, 0, 2)
        give(0, 0, 1)
        near_out(1, 0, 1, 2)
        term(0, 0, 2)
        y_out(1, 1, 0)
        arrives(1, 1, 1)
        y_out(1, 1, 1)
        near_out(1, 1, 0, 2)
        forward(1, 1, 0, 2)
        term(0, 1, 2)
        give(1, 0, 2)
        forward(1, 0, 1, 2)
        arrives(3, 1, 1)
        near_out(3, 1, 0, 1)
        y_out(3, 1, 1)
        near_out(1, 1, 1, 2)
        forward(3, 1, 0, 1)
        pass_on(1, 0, 0, True)
        forward(1, 1, 1, 2)
        arrives(3, 1, 0)
        y_out(3, 1, 0)
        near_out(3, 1, 0, 0)
        give(3, 0, 1)
        forward(3, 1, 0, 0)
        pass_on(1, 0, 1, True)
        arrives(3, 0, 0)
        y_out(3, 0, 0)
        give(3, 0, 0)
        arrives(3, 0, 1)
        near_out(3, 0, 0, 2)
        give(1, 1, 2)
        forward(3, 0, 0, 2)
        near_out(3, 1, 1, 2)
        y_out(3, 0, 1)
        term(3, 0, 2)
        pass_on(3, 0, 0, True)
        forward(3, 1, 1, 2)
        arrives(2, 1, 0)
        y_out(2, 1, 0)
        pass_on(3, 0, 1, True)
        add_beside(0, 0, 0)
        term(1, 1, 2)
        near_out(3, 0, 1, 2)
        arrives(2, 1, 1)
        near_out(2, 1, 0, 2)
        pass_on(1, 1, 0, True)
        y_out(2, 1, 1)
        give(3, 1, 2)
        forward(2, 1, 0, 2)
        arrives(2, 0, 1)
        forward(3, 0, 1, 2)
        give(2, 0, 2)
        term(3, 1, 2)
        add_beside(0, 0, 1)
        arrives(2, 0, 0)
        near_out(2, 0, 0, 2)
        y_out(2, 0, 1)
        y_out(2, 0, 0)
        pass_on(3, 1, 0, True)
        forward(2, 0, 0, 2)
        near_out(2, 1, 1, 2)
        pass_on(3, 1, 1, True)
        finish(0, 0)
        term(2, 0, 2)
        y_out(0, 1, 0)
        forward(2, 1, 1, 2)
        pass_on(2, 0, 0, True)
        near_out(2, 0, 1, 2)
        give(2, 1, 2)
        finish(0, 1)
        forward(2, 0, 1, 2)
        pass_on(2, 0, 1, True)
        near_out(0, 1, 1, 2)
        term(2, 1, 2)
        forward(0, 1, 1, 2)
        pass_on(2, 1, 0, True)
        give(0, 1, 2)
        pass_on(2, 1, 1, True)
        pass_on(1, 1, 1, True)
        add_beside(0, 1, 0)
        finish(1, 0)
        add_beside(0, 1, 1)
        finish(1, 1)
        close()

    for held in (inside, hid_copies, g_copies, kept):
        held.clear()

    @pl.when(is_mid)
    def _():
        own_outer(0, 1)
        forward(0, 0, 0, 2)
        from_x(0)
        y_out(0, 1, 0)
        relay_in(0, 0)
        near_out(0, 1, 0, 0)
        own_outer(1, 0)
        forward(0, 1, 0, 0)
        give(0, 0, 0)
        from_x(1)
        relay_in(0, 1)
        near_out(0, 1, 0, 1)
        own_outer(1, 1)
        y_out(0, 1, 1)
        term(0, 0, 2)
        relay_out(2, 0, 0)
        y_out(2, 0, 0)
        forward(0, 1, 0, 1)
        y_out(3, 0, 1)
        forward(0, 0, 1, 2)
        near_out(3, 0, 0, 2)
        give(0, 0, 1)
        relay_in(1, 1)
        near_out(3, 1, 0, 1)
        near_out(0, 1, 1, 2)
        y_out(3, 0, 0)
        forward(3, 1, 0, 1)
        give(3, 0, 1)
        relay_in(1, 0)
        forward(0, 1, 1, 2)
        near_out(3, 1, 0, 0)
        relay_out(2, 1, 1)
        term(0, 1, 2)
        own_inner(1, 0)
        give(0, 1, 2)
        forward(3, 1, 0, 0)
        relay_out(2, 1, 0)
        y_out(2, 1, 0)
        near_out(2, 1, 0, 2)
        y_out(2, 1, 1)
        relay_out(2, 0, 1)
        near_out(2, 0, 0, 2)
        y_out(2, 0, 1)
        y_out(3, 1, 1)
        forward(3, 0, 0, 2)
        own_inner(1, 1)
        forward(2, 1, 0, 2)
        near_out(3, 0, 1, 2)
        give(3, 0, 0)
        give(2, 0, 2)
        relay_out(1, 1, 0)
        y_out(3, 1, 0)
        own_inner(0, 1)
        forward(2, 0, 0, 2)
        relay_out(1, 1, 1)
        near_out(1, 1, 0, 2)
        y_out(1, 1, 1)
        forward(3, 0, 1, 2)
        term(2, 0, 2)
        add_beside(0, 1, 0)
        y_out(1, 1, 0)
        near_out(2, 1, 1, 2)
        forward(1, 1, 0, 2)
        forward(2, 1, 1, 2)
        term(3, 0, 2)
        relay_out(1, 0, 1)
        near_out(2, 0, 1, 2)
        add_beside(0, 1, 1)
        add_beside(2, 0, 0)
        add_beside(3, 0, 0)
        relay_out(1, 0, 0)
        give(2, 1, 2)
        term(3, 1, 2)
        add_outer(0, 0)
        near_out(1, 0, 0, 2)
        forward(2, 0, 1, 2)
        pass_on(2, 0, 0, False)
        add_beside(2, 0, 1)
        forward(1, 0, 0, 2)
        term(2, 1, 2)
        add_beside(3, 0, 1)
        near_out(3, 1, 1, 2)
        give(1, 0, 2)
        y_out(1, 0, 0)
        pass_on(2, 0, 1, False)
        pass_on(3, 0, 0, False)
        forward(3, 1, 1, 2)
        add_beside(2, 1, 1)
        term(1, 0, 2)
        add_beside(0, 0, 1)
        give(3, 1, 2)
        pass_on(3, 0, 1, False)
        y_out(1, 0, 1)
        add_beside(2, 1, 0)
        pass_on(2, 1, 0, False)
        near_out(1, 1, 1, 2)
        forward(1, 1, 1, 2)
        pass_on(2, 1, 1, False)
        add_beside(1, 0, 0)
        give(1, 1, 2)
        add_beside(1, 0, 1)
        pass_on(1, 0, 0, False)
        near_out(1, 0, 1, 2)
        add_beside(0, 0, 0)
        add_outer(0, 1)
        add_outer(1, 0)
        add_beside(3, 1, 0)
        pass_on(3, 1, 0, False)
        forward(1, 0, 1, 2)
        pass_on(1, 0, 1, False)
        add_beside(3, 1, 1)
        term(1, 1, 2)
        finish(0, 0)
        pass_on(3, 1, 1, False)
        add_beside(1, 1, 0)
        pass_on(1, 1, 0, False)
        finish(0, 1)
        add_beside(1, 1, 1)
        pass_on(1, 1, 1, False)
        finish(1, 0)
        add_outer(1, 1)
        finish(1, 1)
        departed(piece(blk, 0, 0), outer_send.at[blk, 0])
        close()

    for copy in started:
        copy.wait_send()


def cycle_all(tokens, hidden_grad, weights):
    devices = lax.axis_size("blk")
    units, features = weights.shape[1], weights.shape[2]
    token_count = tokens.shape[0]
    part = units // 2
    bf16, f32 = jnp.bfloat16, jnp.float32
    vmem, anywhere = pl.BlockSpec(memory_space=pltpu.VMEM), pl.BlockSpec(memory_space=pl.ANY)
    dma = pltpu.SemaphoreType.DMA
    grads = (2, token_count, part)
    sums = (2, part, features)
    pairs = dma((devices, 2))
    quads = (2, 2, 2)
    return pl.pallas_call(
        cycle_kernel,
        out_shape=(
            jax.ShapeDtypeStruct(hidden_grad.shape, bf16),
            jax.ShapeDtypeStruct((2, units, features), f32),
            jax.ShapeDtypeStruct((2, units, features), f32),
            jax.ShapeDtypeStruct((8, 128), f32),
        ),
        in_specs=[anywhere] * 3,
        out_specs=(anywhere, anywhere, anywhere, vmem),
        scratch_shapes=[
            pltpu.VMEM((2, token_count, features), bf16),
            pltpu.VMEM((token_count, features), bf16),
            pltpu.VMEM(hidden_grad.shape, bf16),
            pltpu.VMEM((2, token_count, part), bf16),
            pltpu.VMEM((devices, 2, units, features), bf16),
            pltpu.VMEM((devices, 2, units, features), bf16),
            pltpu.VMEM((RING,) + grads, bf16),
            pltpu.VMEM((4, 2, 2) + grads, bf16),
            pltpu.VMEM((4, 2) + sums, bf16),
            pltpu.VMEM((4, 2) + sums, bf16),
            pltpu.VMEM((5, 2) + sums, bf16),
            pltpu.VMEM((3, 2) + sums, f32),
            pltpu.VMEM((2, units, features), f32),
            pltpu.VMEM((8, 128), f32),
            pltpu.VMEM((2 * devices, 8, 128), f32),
            dma((4,)), dma((2,)), pairs, pairs, pairs, dma((2,)), pairs, pairs,
            dma((devices, 2, 2)), dma((devices, 2, 2)), dma((2,)),
            dma((4,) + quads), dma((4,) + quads), dma((4,) + quads), dma((4,) + quads), dma((3,) + quads),
            dma((5,) + quads), dma(quads), dma(quads), dma(quads), dma((2 * devices,)), dma((2 * devices,)),
        ],
        compiler_params=pltpu.CompilerParams(
            collective_id=1, has_side_effects=True, vmem_limit_bytes=58 * 1024 * 1024
        ),
    )(tokens, hidden_grad, weights)


def on_ring(tokens, hidden_grad, weights, first_moment, second_moment):
    def partner(value):
        return lax.ppermute(value, "rep", [(0, 1), (1, 0)])

    hidden, gradient, other_gradient, norm_sq = cycle_all(tokens, hidden_grad, weights)
    own = (first_moment, second_moment, weights)
    other = tuple(partner(value) for value in own)
    return adam_all(norm_sq, hidden, (gradient,) + own, (other_gradient,) + other)


def solution(mesh):
    placed = (
        P(("groups", "blk", "rep"), None),
        P(("groups", "blk", "rep"), None),
        P(None, "blk", "rep"),
        P(None, ("groups", "blk"), "rep"),
        P(None, ("groups", "blk"), "rep"),
    )
    devices = mesh.shape["blk"]

    def program(tokens, hidden_grad, weights, first_moment, second_moment):
        slots = hidden_grad.shape[1] * devices // weights.shape[1]
        whole_cycle = slots == devices and devices == 8 and mesh.shape["rep"] == 2 and mesh.shape["groups"] == 2
        step = jax.shard_map(
            on_ring if whole_cycle else on_device,
            mesh=mesh,
            in_specs=placed,
            out_specs=(P(("groups", "blk", "rep"), None), P(None, ("groups", "blk"), None)),
            check_vma=False,
        )
        return step(tokens, hidden_grad, weights, first_moment, second_moment)

    return program
```

```python
import jax
import jax.numpy as jnp
from jax import lax
from jax.experimental import pallas as pl
from jax.experimental.pallas import tpu as pltpu
from jax.sharding import PartitionSpec as P

clip_norm = 1.0
beta_one = 0.9
beta_two = 0.95
step_count = 10.0
adam_eps = 1e-08
decay_rate = 0.1
RING = 6


def shifted(value, axis, by):
    devices = lax.axis_size(axis)
    return lax.ppermute(value, axis, [(i, (i + by) % devices) for i in range(devices)])


def swiglu_terms(tokens, incoming_grad, gate_rows, up_rows):
    contract = (((1,), (1,)), ((), ()))
    gate = lax.dot_general(tokens, gate_rows, contract, preferred_element_type=jnp.float32)
    upper = lax.dot_general(tokens, up_rows, contract, preferred_element_type=jnp.float32)
    sigma = jax.nn.sigmoid(gate)
    activated = gate * sigma
    hidden = (activated * upper).astype(jnp.bfloat16)
    incoming = incoming_grad.astype(jnp.float32)
    gate_grad = (incoming * upper * sigma * (1.0 + gate * (1.0 - sigma))).astype(jnp.bfloat16)
    up_grad = (incoming * activated).astype(jnp.bfloat16)
    return (hidden, gate_grad, up_grad)


def adam_update(gradient, first_moment, second_moment, weights, norm_sq):
    clip_scale = jnp.minimum(1.0, clip_norm / jnp.sqrt(norm_sq))
    clipped = gradient * clip_scale
    first = beta_one * first_moment + (1.0 - beta_one) * clipped
    second = beta_two * second_moment + (1.0 - beta_two) * clipped * clipped
    first_hat = first / (1.0 - beta_one**step_count)
    second_hat = second / (1.0 - beta_two**step_count)
    return first_hat / (jnp.sqrt(second_hat) + adam_eps) + decay_rate * weights.astype(jnp.float32)


def on_device(tokens, hidden_grad, weights, first_moment, second_moment):
    unit_count = weights.shape[1]
    token_count = tokens.shape[0]
    slot_count = hidden_grad.shape[1] // unit_count
    own_full = lax.all_gather(weights, "rep", axis=2, tiled=True)
    slot_grads = jnp.swapaxes(hidden_grad.reshape(token_count, slot_count, unit_count), 0, 1)
    contract = (((1,), (0,)), ((), ()))

    def grad_term(gate_grad, up_grad):
        paired = jnp.stack([gate_grad, up_grad], axis=0)
        return lax.dot_general(paired, tokens, contract, preferred_element_type=jnp.float32)

    zero_sums = jnp.zeros((2, unit_count, tokens.shape[1]), jnp.float32)

    def visit(panel_rows, slot_grad):
        hidden, gate_grad, up_grad = swiglu_terms(tokens, slot_grad, panel_rows[0], panel_rows[1])
        arrived = shifted(panel_rows, "blk", 1)
        return (arrived, (hidden, gate_grad, up_grad))

    _, (hidden_slots, gate_slots, up_slots) = lax.scan(visit, own_full, slot_grads)

    def collect(running, grads_pair):
        arrived = shifted(running, "blk", -1)
        return (arrived + grad_term(grads_pair[0], grads_pair[1]), None)

    owned_sums, _ = lax.scan(collect, zero_sums, (gate_slots, up_slots), reverse=True)
    hidden = jnp.swapaxes(hidden_slots, 0, 1).reshape(token_count, slot_count * unit_count)
    gradient = lax.psum_scatter(owned_sums, "rep", scatter_dimension=2, tiled=True)
    norm_sq = lax.psum(jnp.sum(gradient * gradient), ("blk", "rep"))
    update = adam_update(gradient, first_moment, second_moment, weights, norm_sq)
    adam_step = lax.all_gather(update, "rep", axis=2, tiled=True)
    return (hidden, adam_step)


def adam_kernel(
    norm_hbm, hidden_hbm, grad_hbm, near_grad_hbm, first_hbm, second_hbm, weights_hbm, near_first_hbm, near_second_hbm,
    near_weights_hbm, hidden_out, step_out, norm, grad, first_moment, second_moment, weights, update, hidden, norm_sem,
    load_sem, hid_sem, move_sem, store_sem
):
    units, features = grad.shape[2], grad.shape[3]
    tile = units // 4
    sources = (
        (grad_hbm, first_hbm, second_hbm, weights_hbm),
        (near_grad_hbm, near_first_hbm, near_second_hbm, near_weights_hbm),
    )
    held = (grad, first_moment, second_moment, weights)
    steps = [(which, pl.ds(at, tile)) for which in range(2) for at in range(0, units, tile)]
    norm_copy = pltpu.make_async_copy(norm_hbm, norm, norm_sem)
    norm_copy.start()
    loads = []
    for i, (which, rows) in enumerate(steps):
        loads.append([])
        for side in range(2):
            for j in range(4):
                copy = pltpu.make_async_copy(
                    sources[side][j].at[which, rows], held[j].at[side, which, rows], load_sem.at[i, side, j]
                )
                copy.start()
                loads[-1].append(copy)
    band = hidden_hbm.shape[0] // 8
    bands = [pl.ds(i * band, band) for i in range(8)]
    brought = [pltpu.make_async_copy(hidden_hbm.at[rows], hidden.at[rows], hid_sem.at[i]) for i, rows in enumerate(bands)]
    moved = [pltpu.make_async_copy(hidden.at[rows], hidden_out.at[rows], move_sem.at[i]) for i, rows in enumerate(bands)]
    for copy in brought:
        copy.start()
    rep = lax.axis_index("rep")
    columns = [pl.ds(pl.multiple_of(at * features, features), features) for at in (rep, 1 - rep)]
    norm_copy.wait()
    scale = jnp.minimum(1.0, clip_norm / jnp.sqrt(norm[0:1, 0:1]))
    stores = []
    for i, (which, rows) in enumerate(steps):
        for side in range(2):
            for copy in loads[i][4 * side : 4 * side + 4]:
                copy.wait()

            @pl.loop(0, tile // 16)
            def _(t):
                at = pl.ds(pl.multiple_of(rows.start + t * 16, 16), 16)
                clipped = grad[side, which, at, :] * scale
                moment = beta_one * first_moment[side, which, at, :] + (1.0 - beta_one) * clipped
                square = beta_two * second_moment[side, which, at, :] + (1.0 - beta_two) * clipped * clipped
                moment = moment * (1.0 / (1.0 - beta_one**step_count))
                square = square * (1.0 / (1.0 - beta_two**step_count))
                decay = decay_rate * weights[side, which, at, :].astype(jnp.float32)
                update[which, at, columns[side]] = moment / (square * lax.rsqrt(square) + adam_eps) + decay

        stores.append(pltpu.make_async_copy(update.at[which, rows], step_out.at[which, rows], store_sem.at[i]))
        stores[-1].start()
        brought[i].wait()
        moved[i].start()
    for copy in moved + stores:
        copy.wait()


def adam_all(norm_sq, hidden, own, other):
    pair, units, features = own[0].shape
    f32, dma = jnp.float32, pltpu.SemaphoreType.DMA
    anywhere = pl.BlockSpec(memory_space=pl.ANY)
    hbm = pl.BlockSpec(memory_space=pltpu.HBM)
    both = (2, pair, units, features)
    return pl.pallas_call(
        adam_kernel,
        out_shape=(
            jax.ShapeDtypeStruct(hidden.shape, hidden.dtype),
            jax.ShapeDtypeStruct((pair, units, 2 * features), f32),
        ),
        in_specs=[hbm, hbm, hbm, hbm] + [anywhere] * 6,
        out_specs=(hbm, hbm),
        scratch_shapes=[
            pltpu.VMEM((8, 128), f32),
            pltpu.VMEM(both, f32),
            pltpu.VMEM(both, f32),
            pltpu.VMEM(both, f32),
            pltpu.VMEM(both, jnp.bfloat16),
            pltpu.VMEM((pair, units, 2 * features), f32),
            pltpu.VMEM(hidden.shape, hidden.dtype),
            dma, dma((8, 2, 4)), dma((8,)), dma((8,)), dma((8,)),
        ],
        compiler_params=pltpu.CompilerParams(vmem_limit_bytes=63 * 1024 * 1024),
    )(norm_sq, hidden, own[0], other[0], own[1], own[2], own[3], other[1], other[2], other[3])


def cycle_kernel(
    tokens_hbm, grad_hbm, weights_hbm, hidden_hbm, sum_hbm, other_sum, norm_ref,
    tok, tok_near, incoming_ref, hid, mine, other, grads_out, grads_in, x_out, x_in, z_in, sums, own_sum, squares, slots,
    load_sem, hid_sem, ag_recv, inner_send, outer_send, x_send, y_send, y_recv, near_send, near_recv, tok_sem,
    g_send, g_recv, xr_send, xr_recv, zr_send, zr_recv, swap_send, swap_recv, sum_sem, norm_send, norm_recv
):
    devices = lax.axis_size("blk")
    units, features = weights_hbm.shape[1], weights_hbm.shape[2]
    token_count = tok.shape[1]
    part = units // 2
    step = part // 2
    blk, rep, group = lax.axis_index("blk"), lax.axis_index("rep"), lax.axis_index("groups")
    z, x = blk // 2, blk % 2
    end = 1 - ((z + 1) // 2) % 2
    turn = 1 - 2 * (z // 2)
    is_end, is_mid = end == 1, end == 0
    mesh_ids = pl.DeviceIdType.MESH
    near = {"rep": 1 - rep}
    across = {"groups": 1 - group}
    beside = {"blk": 2 * z + 1 - x}
    inner = {"blk": 2 * (z + turn) + x}
    outer = {"blk": 2 * (z - turn * (1 - end)) + x}
    third_z = z + turn * (4 * end - 1)

    def panel(visit, col):
        at = z + turn * visit if visit < 3 else third_z
        return 2 * at + (x if col == 0 else 1 - x)

    row_at = [pl.multiple_of(group * part, part), pl.multiple_of((1 - group) * part, part)]

    def rows_of(half, sub):
        if sub == 2:
            return pl.ds(row_at[half], part)
        return pl.ds(pl.multiple_of(row_at[half] + sub * step, step), step)

    def within(sub):
        return pl.ds(0, part) if sub == 2 else pl.ds(sub * step, step)

    own_at = pl.multiple_of(rep * features, features)
    other_at = pl.multiple_of((1 - rep) * features, features)

    loads = [
        pltpu.make_async_copy(tokens_hbm.at[:, pl.ds(own_at, features)], tok.at[0], load_sem.at[0]),
        pltpu.make_async_copy(tokens_hbm.at[:, pl.ds(other_at, features)], tok.at[1], load_sem.at[1]),
        pltpu.make_async_copy(weights_hbm, mine.at[blk], load_sem.at[2]),
        pltpu.make_async_copy(grad_hbm, incoming_ref, load_sem.at[3]),
    ]
    for copy in loads:
        copy.start()

    members = 2 * devices
    me = blk * 2 + rep

    def member(by):
        peer = (me + by) % members
        return {"blk": peer // 2, "rep": peer % 2}

    barrier = pltpu.get_barrier_semaphore()
    for by in range(1, members):
        pl.semaphore_signal(barrier, inc=1, device_id=member(by), device_id_type=mesh_ids)
    pl.semaphore_signal(barrier, inc=1, device_id=across, device_id_type=mesh_ids)
    pl.semaphore_wait(barrier, members)

    started, inside = [], []

    def send(source, target, send_sem, recv_sem, peer, keep=None):
        copy = pltpu.make_async_remote_copy(
            src_ref=source, dst_ref=target, send_sem=send_sem, recv_sem=recv_sem, device_id=peer, device_id_type=mesh_ids
        )
        copy.start()
        if keep is not None:
            keep.append(copy)
        return copy

    def arrive(target, sem, peer):
        pltpu.make_async_remote_copy(
            src_ref=target, dst_ref=target, send_sem=sem, recv_sem=sem, device_id=peer, device_id_type=mesh_ids
        ).wait_recv()

    def departed(ref, sem):
        pltpu.make_async_remote_copy(
            src_ref=ref, dst_ref=ref, send_sem=sem, recv_sem=sem, device_id=inner, device_id_type=mesh_ids
        ).wait_send()

    def piece(q, half, sub):
        return mine.at[q, :, rows_of(half, sub)]

    def own_piece(sub):
        return weights_hbm.at[:, rows_of(0, sub)]

    def line_send(outward, visit, col, sub, keep=inside):
        q = panel(visit, col)
        source = own_piece(sub) if visit == 0 and col == 0 else piece(q, 0, sub)
        sems = outer_send if outward else inner_send
        send(source, piece(q, 0, sub), sems.at[q, sub], ag_recv.at[q, sub], outer if outward else inner, keep)

    def wait_piece(q, sub):
        arrive(piece(q, 0, sub), ag_recv.at[q, sub], inner)

    def from_x(sub):
        wait_piece(panel(0, 1), sub)

    def own_inner(col, sub):
        line_send(False, 0, col, sub)

    def own_outer(col, sub):
        line_send(True, 0, col, sub)

    def arrives(visit, col, sub):
        wait_piece(panel(visit, col), sub)

    def relay_out(visit, col, sub):
        wait_piece(panel(visit, col), sub)
        line_send(True, visit, col, sub)

    def relay_in(col, sub):
        wait_piece(panel(3, col), sub)
        line_send(False, 3, col, sub)

    def y_out(visit, col, sub):
        q = panel(visit, col)
        send(piece(q, 0, sub), piece(q, 0, sub), y_send.at[q, sub], y_recv.at[q, sub], across, inside)

    def near_out(visit, col, half, sub):
        q = panel(visit, col)
        if half == 1:
            for i in (0, 1) if sub == 2 else (sub,):
                arrive(piece(q, 1, i), y_recv.at[q, i], across)
        rows = rows_of(half, sub)
        send(
            mine.at[q, :, rows], other.at[q, :, rows], near_send.at[q, half, sub % 2], near_recv.at[q, half, sub % 2],
            near, inside,
        )

    tile = min(token_count, 128)
    across_features = (((1,), (1,)), ((), ()))
    across_tokens = (((0,), (0,)), ((), ()))
    hid_copies, g_copies, kept, ring_at = [], [], [], {}
    ring = grads_out.shape[0]

    def forward(visit, col, half, sub):
        q = panel(visit, col)
        unit_rows, cut = rows_of(half, sub), within(sub)
        arrive(other.at[q, :, unit_rows], near_recv.at[q, half, sub % 2], near)
        slot = (blk - q + devices) % devices
        columns = pl.ds(pl.multiple_of(slot * units + unit_rows.start, 128), unit_rows.size)
        if len(hid_copies) >= 2:
            hid_copies[-2].wait()
        stage = hid.at[len(hid_copies) % 2, :, cut]
        if len(g_copies) >= ring:
            g_copies[-ring].wait_send()
        for i in (0, 1) if sub == 2 else (sub,):
            ring_at[visit, col, half, i] = len(g_copies) % ring
        grads = grads_out.at[len(g_copies) % ring, :, :, cut]

        @pl.loop(0, token_count // tile)
        def _(t):
            rows = pl.ds(pl.multiple_of(t * tile, tile), tile)
            own_tokens, other_tokens = tok[0, rows, :], tok[1, rows, :]

            def product(which):
                return lax.dot_general(
                    own_tokens, mine[q, which, unit_rows, :], across_features, preferred_element_type=jnp.float32
                ) + lax.dot_general(
                    other_tokens, other[q, which, unit_rows, :], across_features, preferred_element_type=jnp.float32
                )

            gate, upper = product(0), product(1)
            incoming = incoming_ref[rows, columns].astype(jnp.float32)
            sigma = jax.nn.sigmoid(gate)
            activated = gate * sigma
            stage[rows, :] = (activated * upper).astype(jnp.bfloat16)
            grads[0, rows, :] = (incoming * upper * sigma * (1.0 + gate * (1.0 - sigma))).astype(jnp.bfloat16)
            grads[1, rows, :] = (incoming * activated).astype(jnp.bfloat16)

        copy = pltpu.make_async_copy(stage, hidden_hbm.at[:, columns], hid_sem.at[len(hid_copies) % 2])
        copy.start()
        hid_copies.append(copy)
        send(
            grads, grads_in.at[visit, col, half, :, :, cut], g_send.at[visit, col, half, sub % 2],
            g_recv.at[visit, col, half, sub % 2], near, g_copies,
        )

    def got_grads(visit, col, half, sub):
        arrive(grads_in.at[visit, col, half, :, :, within(sub)], g_recv.at[visit, col, half, sub % 2], near)

    def gradient_term(visit, col, half, sub, which):
        grads = grads_out.at[ring_at[visit, col, half, sub % 2]]
        got = grads_in.at[visit, col, half]
        rows = within(sub)
        return lax.dot_general(
            grads[which, :, rows], tok[0], across_tokens, preferred_element_type=jnp.float32
        ) + lax.dot_general(got[which, :, rows], tok_near[...], across_tokens, preferred_element_type=jnp.float32)

    def give(visit, half, sub):
        got_grads(visit, 1, half, sub)
        for i in (0, 1) if sub == 2 else (sub,):
            for which in range(2):
                target = x_out.at[visit, half, which, within(i)]
                target[...] = gradient_term(visit, 1, half, i, which).astype(jnp.bfloat16)
                send(
                    target, x_in.at[visit, half, which, within(i)], xr_send.at[visit, half, i, which],
                    xr_recv.at[visit, half, i, which], beside, inside,
                )

    def total_at(visit, half, which, sub):
        if visit == 0:
            return own_sum.at[which, rows_of(half, sub)]
        return sums.at[visit - 1, half, which, within(sub)]

    def term(visit, half, sub):
        got_grads(visit, 0, half, sub)
        for which in range(2):
            total_at(visit, half, which, sub)[...] = gradient_term(visit, 0, half, sub, which)

    def from_beside(visit, half, sub, which):
        arrive(x_in.at[visit, half, which, within(sub)], xr_recv.at[visit, half, sub, which], beside)
        return x_in[visit, half, which, within(sub), :].astype(jnp.float32)

    def from_line(slot, half, sub, which):
        arrive(z_in.at[slot, half, which, within(sub)], zr_recv.at[slot, half, sub, which], inner)
        return z_in[slot, half, which, within(sub), :].astype(jnp.float32)

    def add_beside(visit, half, sub):
        for which in range(2):
            total_at(visit, half, which, sub)[...] += from_beside(visit, half, sub, which)

    def add_outer(half, sub):
        for which in range(2):
            total_at(0, half, which, sub)[...] += from_line(0, half, sub, which)

    def pass_on(visit, half, sub, at_end):
        to = visit - 1 if at_end else 3 + visit % 2
        peer = outer if visit == 3 and not at_end else inner
        for which in range(2):
            if at_end:
                added = from_beside(visit, half, sub, which)
            else:
                added = from_line(visit, half, sub, which)
            target = x_in.at[visit, half, which, within(sub)]
            target[...] = (total_at(visit, half, which, sub)[...] + added).astype(jnp.bfloat16)
            send(
                target, z_in.at[to, half, which, within(sub)], zr_send.at[visit - 1, half, sub, which],
                zr_recv.at[to, half, sub, which], peer, inside,
            )

    def finish(half, sub):
        for which in range(2):
            target = total_at(0, half, which, sub)
            total = target[...] + from_line(4, half, sub, which)
            target[...] = total
            folded = jnp.sum((total * total).reshape(step // 8, 8, features), axis=0)
            for lane in range(0, features, 128):
                squares[...] += folded[:, lane : lane + 128]
            rows = rows_of(half, sub)
            send(
                target, other_sum.at[which, rows], swap_send.at[half, sub, which], swap_recv.at[half, sub, which], near,
                inside,
            )
            copy = pltpu.make_async_copy(target, sum_hbm.at[which, rows], sum_sem.at[half, sub, which])
            copy.start()
            kept.append(copy)

    def own_start(sub):
        send(own_piece(sub), piece(blk, 0, sub), x_send.at[sub], ag_recv.at[blk, sub], beside, started)

    own_start(0)
    line_send(False, 0, 0, 0, started)

    @pl.when(is_mid)
    def _():
        line_send(True, 0, 0, 0, None)

    own_start(1)
    for half in range(2):
        rows = rows_of(half, 2)
        send(
            weights_hbm.at[:, rows], other.at[blk, :, rows], near_send.at[blk, half, 0], near_recv.at[blk, half, 0], near,
            started,
        )
    loads[1].wait()
    send(tok.at[1], tok_near, tok_sem.at[0], tok_sem.at[1], near, started)
    squares[...] = jnp.zeros_like(squares)
    for copy in (loads[0], loads[2], loads[3]):
        copy.wait()
    arrive(tok_near, tok_sem.at[1], near)

    def close():
        slots[me] = squares[...]
        copies = []
        for by in range(1, members):
            send(squares, slots.at[me], norm_send.at[by], norm_recv.at[by], member(by), copies)
        for copy in inside + g_copies[-ring:]:
            copy.wait_send()
        for copy in hid_copies[-2:] + kept:
            copy.wait()
        for half in range(2):
            for sub in range(2):
                for which in range(2):
                    arrive(other_sum.at[which, rows_of(half, sub)], swap_recv.at[half, sub, which], near)
        for copy in copies:
            copy.wait()
        total = slots[0]
        for i in range(1, members):
            total = total + slots[i]
        norm_ref[...] = jnp.full(norm_ref.shape, jnp.sum(total), jnp.float32)

    @pl.when(is_end)
    def _():
        own_inner(0, 1)
        forward(0, 0, 0, 2)
        forward(0, 0, 1, 2)
        arrives(1, 0, 0)
        y_out(1, 0, 0)
        from_x(0)
        near_out(0, 1, 0, 0)
        forward(0, 1, 0, 0)
        from_x(1)
        own_inner(1, 1)
        arrives(1, 0, 1)
        y_out(1, 0, 1)
        near_out(0, 1, 0, 1)
        own_inner(1, 0)
        near_out(1, 0, 0, 2)
        give(0, 0, 0)
        forward(0, 1, 0, 1)
        forward(1, 0, 0, 2)
        arrives(1, 1, 0)
        y_out(0, 1, 1)
        term(1, 0, 2)
        give(0, 0, 1)
        near_out(1, 0, 1, 2)
        term(0, 0, 2)
        y_out(1, 1, 0)
        arrives(1, 1, 1)
        y_out(1, 1, 1)
        near_out(1, 1, 0, 2)
        forward(1, 1, 0, 2)
        term(0, 1, 2)
        give(1, 0, 2)
        forward(1, 0, 1, 2)
        arrives(3, 1, 1)
        near_out(3, 1, 0, 1)
        y_out(3, 1, 1)
        near_out(1, 1, 1, 2)
        forward(3, 1, 0, 1)
        pass_on(1, 0, 0, True)
        forward(1, 1, 1, 2)
        arrives(3, 1, 0)
        y_out(3, 1, 0)
        near_out(3, 1, 0, 0)
        give(3, 0, 1)
        forward(3, 1, 0, 0)
        pass_on(1, 0, 1, True)
        arrives(3, 0, 0)
        y_out(3, 0, 0)
        give(3, 0, 0)
        arrives(3, 0, 1)
        near_out(3, 0, 0, 2)
        give(1, 1, 2)
        forward(3, 0, 0, 2)
        near_out(3, 1, 1, 2)
        y_out(3, 0, 1)
        term(3, 0, 2)
        pass_on(3, 0, 0, True)
        forward(3, 1, 1, 2)
        arrives(2, 1, 0)
        y_out(2, 1, 0)
        pass_on(3, 0, 1, True)
        add_beside(0, 0, 0)
        term(1, 1, 2)
        near_out(3, 0, 1, 2)
        arrives(2, 1, 1)
        near_out(2, 1, 0, 2)
        pass_on(1, 1, 0, True)
        y_out(2, 1, 1)
        give(3, 1, 2)
        forward(2, 1, 0, 2)
        arrives(2, 0, 1)
        forward(3, 0, 1, 2)
        give(2, 0, 2)
        term(3, 1, 2)
        add_beside(0, 0, 1)
        arrives(2, 0, 0)
        near_out(2, 0, 0, 2)
        y_out(2, 0, 1)
        y_out(2, 0, 0)
        pass_on(3, 1, 0, True)
        forward(2, 0, 0, 2)
        near_out(2, 1, 1, 2)
        pass_on(3, 1, 1, True)
        finish(0, 0)
        term(2, 0, 2)
        y_out(0, 1, 0)
        forward(2, 1, 1, 2)
        pass_on(2, 0, 0, True)
        near_out(2, 0, 1, 2)
        give(2, 1, 2)
        finish(0, 1)
        forward(2, 0, 1, 2)
        pass_on(2, 0, 1, True)
        near_out(0, 1, 1, 2)
        term(2, 1, 2)
        forward(0, 1, 1, 2)
        pass_on(2, 1, 0, True)
        give(0, 1, 2)
        pass_on(2, 1, 1, True)
        pass_on(1, 1, 1, True)
        add_beside(0, 1, 0)
        finish(1, 0)
        add_beside(0, 1, 1)
        finish(1, 1)
        close()

    for held in (inside, hid_copies, g_copies, kept):
        held.clear()

    @pl.when(is_mid)
    def _():
        own_outer(0, 1)
        forward(0, 0, 0, 2)
        from_x(0)
        y_out(0, 1, 0)
        relay_in(0, 0)
        near_out(0, 1, 0, 0)
        own_outer(1, 0)
        forward(0, 1, 0, 0)
        give(0, 0, 0)
        from_x(1)
        relay_in(0, 1)
        near_out(0, 1, 0, 1)
        own_outer(1, 1)
        y_out(0, 1, 1)
        term(0, 0, 2)
        relay_out(2, 0, 0)
        y_out(2, 0, 0)
        forward(0, 1, 0, 1)
        y_out(3, 0, 1)
        forward(0, 0, 1, 2)
        near_out(3, 0, 0, 2)
        give(0, 0, 1)
        relay_in(1, 1)
        near_out(3, 1, 0, 1)
        near_out(0, 1, 1, 2)
        y_out(3, 0, 0)
        forward(3, 1, 0, 1)
        give(3, 0, 1)
        relay_in(1, 0)
        forward(0, 1, 1, 2)
        near_out(3, 1, 0, 0)
        relay_out(2, 1, 1)
        term(0, 1, 2)
        own_inner(1, 0)
        give(0, 1, 2)
        forward(3, 1, 0, 0)
        relay_out(2, 1, 0)
        y_out(2, 1, 0)
        near_out(2, 1, 0, 2)
        y_out(2, 1, 1)
        relay_out(2, 0, 1)
        near_out(2, 0, 0, 2)
        y_out(2, 0, 1)
        y_out(3, 1, 1)
        forward(3, 0, 0, 2)
        own_inner(1, 1)
        forward(2, 1, 0, 2)
        near_out(3, 0, 1, 2)
        give(3, 0, 0)
        give(2, 0, 2)
        relay_out(1, 1, 0)
        y_out(3, 1, 0)
        own_inner(0, 1)
        forward(2, 0, 0, 2)
        relay_out(1, 1, 1)
        near_out(1, 1, 0, 2)
        y_out(1, 1, 1)
        forward(3, 0, 1, 2)
        term(2, 0, 2)
        add_beside(0, 1, 0)
        y_out(1, 1, 0)
        near_out(2, 1, 1, 2)
        forward(1, 1, 0, 2)
        forward(2, 1, 1, 2)
        term(3, 0, 2)
        relay_out(1, 0, 1)
        near_out(2, 0, 1, 2)
        add_beside(0, 1, 1)
        add_beside(2, 0, 0)
        add_beside(3, 0, 0)
        relay_out(1, 0, 0)
        give(2, 1, 2)
        term(3, 1, 2)
        add_outer(0, 0)
        near_out(1, 0, 0, 2)
        forward(2, 0, 1, 2)
        pass_on(2, 0, 0, False)
        add_beside(2, 0, 1)
        forward(1, 0, 0, 2)
        term(2, 1, 2)
        add_beside(3, 0, 1)
        near_out(3, 1, 1, 2)
        give(1, 0, 2)
        y_out(1, 0, 0)
        pass_on(2, 0, 1, False)
        pass_on(3, 0, 0, False)
        forward(3, 1, 1, 2)
        add_beside(2, 1, 1)
        term(1, 0, 2)
        add_beside(0, 0, 1)
        give(3, 1, 2)
        pass_on(3, 0, 1, False)
        y_out(1, 0, 1)
        add_beside(2, 1, 0)
        pass_on(2, 1, 0, False)
        near_out(1, 1, 1, 2)
        forward(1, 1, 1, 2)
        pass_on(2, 1, 1, False)
        add_beside(1, 0, 0)
        give(1, 1, 2)
        add_beside(1, 0, 1)
        pass_on(1, 0, 0, False)
        near_out(1, 0, 1, 2)
        add_beside(0, 0, 0)
        add_outer(0, 1)
        add_outer(1, 0)
        add_beside(3, 1, 0)
        pass_on(3, 1, 0, False)
        forward(1, 0, 1, 2)
        pass_on(1, 0, 1, False)
        add_beside(3, 1, 1)
        term(1, 1, 2)
        finish(0, 0)
        pass_on(3, 1, 1, False)
        add_beside(1, 1, 0)
        pass_on(1, 1, 0, False)
        finish(0, 1)
        add_beside(1, 1, 1)
        pass_on(1, 1, 1, False)
        finish(1, 0)
        add_outer(1, 1)
        finish(1, 1)
        departed(piece(blk, 0, 0), outer_send.at[blk, 0])
        close()

    for copy in started:
        copy.wait_send()


def cycle_all(tokens, hidden_grad, weights):
    devices = lax.axis_size("blk")
    units, features = weights.shape[1], weights.shape[2]
    token_count = tokens.shape[0]
    part = units // 2
    bf16, f32 = jnp.bfloat16, jnp.float32
    vmem, anywhere = pl.BlockSpec(memory_space=pltpu.VMEM), pl.BlockSpec(memory_space=pl.ANY)
    dma = pltpu.SemaphoreType.DMA
    grads = (2, token_count, part)
    sums = (2, part, features)
    pairs = dma((devices, 2))
    quads = (2, 2, 2)
    return pl.pallas_call(
        cycle_kernel,
        out_shape=(
            jax.ShapeDtypeStruct(hidden_grad.shape, bf16),
            jax.ShapeDtypeStruct((2, units, features), f32),
            jax.ShapeDtypeStruct((2, units, features), f32),
            jax.ShapeDtypeStruct((8, 128), f32),
        ),
        in_specs=[anywhere] * 3,
        out_specs=(anywhere, anywhere, anywhere, vmem),
        scratch_shapes=[
            pltpu.VMEM((2, token_count, features), bf16),
            pltpu.VMEM((token_count, features), bf16),
            pltpu.VMEM(hidden_grad.shape, bf16),
            pltpu.VMEM((2, token_count, part), bf16),
            pltpu.VMEM((devices, 2, units, features), bf16),
            pltpu.VMEM((devices, 2, units, features), bf16),
            pltpu.VMEM((RING,) + grads, bf16),
            pltpu.VMEM((4, 2, 2) + grads, bf16),
            pltpu.VMEM((4, 2) + sums, bf16),
            pltpu.VMEM((4, 2) + sums, bf16),
            pltpu.VMEM((5, 2) + sums, bf16),
            pltpu.VMEM((3, 2) + sums, f32),
            pltpu.VMEM((2, units, features), f32),
            pltpu.VMEM((8, 128), f32),
            pltpu.VMEM((2 * devices, 8, 128), f32),
            dma((4,)), dma((2,)), pairs, pairs, pairs, dma((2,)), pairs, pairs,
            dma((devices, 2, 2)), dma((devices, 2, 2)), dma((2,)),
            dma((4,) + quads), dma((4,) + quads), dma((4,) + quads), dma((4,) + quads), dma((3,) + quads),
            dma((5,) + quads), dma(quads), dma(quads), dma(quads), dma((2 * devices,)), dma((2 * devices,)),
        ],
        compiler_params=pltpu.CompilerParams(
            collective_id=1, has_side_effects=True, vmem_limit_bytes=58 * 1024 * 1024
        ),
    )(tokens, hidden_grad, weights)


def on_ring(tokens, hidden_grad, weights, first_moment, second_moment):
    def partner(value):
        return lax.ppermute(value, "rep", [(0, 1), (1, 0)])

    hidden, gradient, other_gradient, norm_sq = cycle_all(tokens, hidden_grad, weights)
    own = (first_moment, second_moment, weights)
    other = tuple(partner(value) for value in own)
    return adam_all(norm_sq, hidden, (gradient,) + own, (other_gradient,) + other)


def solution(mesh):
    placed = (
        P(("groups", "blk", "rep"), None),
        P(("groups", "blk", "rep"), None),
        P(None, "blk", "rep"),
        P(None, ("groups", "blk"), "rep"),
        P(None, ("groups", "blk"), "rep"),
    )
    devices = mesh.shape["blk"]

    def program(tokens, hidden_grad, weights, first_moment, second_moment):
        slots = hidden_grad.shape[1] * devices // weights.shape[1]
        whole_cycle = slots == devices and devices == 8 and mesh.shape["rep"] == 2 and mesh.shape["groups"] == 2
        step = jax.shard_map(
            on_ring if whole_cycle else on_device,
            mesh=mesh,
            in_specs=placed,
            out_specs=(P(("groups", "blk", "rep"), None), P(None, ("groups", "blk"), None)),
            check_vma=False,
        )
        return step(tokens, hidden_grad, weights, first_moment, second_moment)

    return program
```
